32 devices in a mesh: atlas: 4 (over y, x), row: 2 (over core), col: 4 (over z).
Axes of the slice: x: 2, y: 2, z: 4, core: 2. Of those that a mesh axis runs over, the one named last changes fastest.
Arguments:
- cells: bfloat16 [4, 64, 1024], P('atlas', None, 'row'), may hold values from -4 to 4
- support: bfloat16 [64, 16384], P(None, 'col'), may hold values from -4 to 4
Outputs:
- cell_dual: float32 [4, 1024], P('atlas', 'row')
- support_dual: float32 [4, 16384], P('atlas', 'col')
- new_support: float32 [64, 16384], P(None, 'col')
The draws below stay inside these ranges and needn't reach their ends.
All inputs are finite; a program needn't handle non-finite values.
Results may differ from the reference program's by a relative error of at most 0.001.
Values sent between devices are 32-bit elements; how exact they have to be, the bound alone decides.
No kernel may reach another device: no remote copies, remote signals or barrier semaphores. Data moves between devices by JAX's collectives and lax.ppermute only.
A program may use at most 64 MiB of HBM per device.

```python
import jax
import jax.numpy as jnp
from jax import lax

D = 64
SUPPORT = 16384
ITERS = 2
CELLS = 1024
ATLASES = 4


def draw_cells(key, part):
    own_key = jax.random.fold_in(key, 1)
    values = jax.random.truncated_normal(own_key, -4.0, 4.0, (ATLASES, D, CELLS), jnp.float32)
    return values.astype(jnp.bfloat16)


def draw_support(key, part):
    own_key = jax.random.fold_in(key, 2)
    values = jax.random.truncated_normal(own_key, -4.0, 4.0, (D, SUPPORT), jnp.float32)
    return values.astype(jnp.bfloat16)


def setup_inputs(seed: int = 0) -> dict:
    seeds = jax.random.split(jax.random.key(seed), 3)
    cells = draw_cells(jax.random.fold_in(seeds[2], 71), 0)
    support = draw_support(jax.random.fold_in(seeds[2], 71), 0)
    return dict(cells=cells, support=support)


blur = 0.1


def reference(cells, support):
    dims = support.shape[0]
    total_support = support.shape[1]
    total_cells = cells.shape[2]
    atlases = cells.shape[0]
    width_block = min(512, total_support)
    count = total_support // width_block
    support_blocks = support.reshape(dims, count, width_block).transpose(1, 0, 2)
    squares_y = jnp.sum(jnp.square(support.astype(jnp.float32)), axis=0).reshape(count, width_block)
    duals_f = []
    duals_g = []
    summed = jnp.zeros((dims, total_support), jnp.float32)
    for atlas in range(atlases):
        points = cells[atlas]
        points_wide = points.astype(jnp.float32)
        squares_x = jnp.sum(jnp.square(points_wide), axis=0)

        def tile_cost(piece, near):
            cross = lax.dot_general(points, piece, (((0,), (0,)), ((), ())), preferred_element_type=jnp.float32)
            return (squares_x[:, None] + near[None, :] - 2.0 * cross) / dims

        dual_g = jnp.zeros((count, width_block), jnp.float32)
        dual_f = jnp.zeros((total_cells,), jnp.float32)
        for step in range(ITERS):
            def visit(carry, item):
                top, total = carry
                piece, near, gpart = item
                logits = (gpart[None, :] - tile_cost(piece, near)) / blur
                peak = jnp.maximum(top, jnp.max(logits, axis=1))
                total = total * jnp.exp(top - peak) + jnp.sum(jnp.exp(logits - peak[:, None]), axis=1)
                return (peak, total), None

            start_carry = (jnp.full((total_cells,), -jnp.inf, jnp.float32), jnp.zeros((total_cells,), jnp.float32))
            (top, total), unused = lax.scan(visit, start_carry, (support_blocks, squares_y, dual_g))
            dual_f = blur * jnp.log(1.0 / total_cells) - blur * (top + jnp.log(total))

            def column(item):
                piece, near = item
                logits = (dual_f[:, None] - tile_cost(piece, near)) / blur
                peak = jnp.max(logits, axis=0)
                mass = jnp.sum(jnp.exp(logits - peak[None, :]), axis=0)
                return blur * jnp.log(1.0 / total_support) - blur * (peak + jnp.log(mass))

            dual_g = lax.map(column, (support_blocks, squares_y))

        def weigh(item):
            piece, near, gpart = item
            plan = jnp.exp((dual_f[:, None] + gpart[None, :] - tile_cost(piece, near)) / blur)
            return jnp.dot(points_wide, plan, precision=lax.Precision.HIGHEST) * total_support

        terms = lax.map(weigh, (support_blocks, squares_y, dual_g))
        summed = summed + terms.transpose(1, 0, 2).reshape(dims, total_support)
        duals_f.append(dual_f)
        duals_g.append(dual_g.reshape(total_support))
    return jnp.stack(duals_f), jnp.stack(duals_g), summed / atlases
```

```python
import functools
import math

import jax
import jax.numpy as jnp
from jax import lax
from jax.experimental import pallas as pl
from jax.experimental.pallas import tpu as pltpu
from jax.sharding import PartitionSpec as P


ITERS = 2
blur = 0.1
LANES = 128
SUBLANES = 8
LOG2E = 1.4426950408889634
VMEM = pl.BlockSpec(memory_space=pltpu.VMEM)


def pieces(value):
    high = value.astype(jnp.bfloat16)
    rest = value - high.astype(jnp.float32)
    mid = rest.astype(jnp.bfloat16)
    low = (rest - mid.astype(jnp.float32)).astype(jnp.bfloat16)
    return high, mid, low


def pad_rows(rows, count):
    width = rows[0].shape[1]
    index = lax.broadcasted_iota(jnp.int32, (16, width), 0)
    block = jnp.zeros((16, width), jnp.float32)
    for at, row in enumerate(rows):
        block = jnp.where(index == at, row.astype(jnp.float32), block)
    return block.astype(jnp.bfloat16)


def ones_rows(width):
    index = lax.broadcasted_iota(jnp.int32, (16, width), 0)
    return jnp.where(index < 3, 1.0, 0.0).astype(jnp.bfloat16)


def lane_tiles(width):
    return [slice(at, at + LANES) for at in range(0, width, LANES)]


def first_kernel(scale, x_ref, y_ref, out_ref, left, right, logits, tops, sums):
    dims, rows = x_ref.shape
    columns = y_ref.shape[1]
    block = min(512, columns)
    wide = x_ref[...].astype(jnp.float32) * (2.0 * scale)
    left[...] = jnp.concatenate([*pieces(wide), ones_rows(rows)], axis=0).T
    for start in range(0, columns, block):
        piece = y_ref[:, start : start + block]
        near = jnp.sum(jnp.square(piece.astype(jnp.float32)), axis=0, keepdims=True)
        right[:, start : start + block] = jnp.concatenate(
            [piece, piece, piece, pad_rows(pieces(-scale * near), 3)], axis=0
        )
    for start in range(0, columns, block):
        part = jnp.dot(
            left[...], right[:, start : start + block], preferred_element_type=jnp.float32
        )
        logits[:, start : start + block] = part
        top = functools.reduce(jnp.maximum, [part[:, tile] for tile in lane_tiles(block)])
        tops[...] = top if start == 0 else jnp.maximum(tops[...], top)
    height = min(64, rows)
    for low in range(0, rows, height):
        span = slice(low, low + height)
        top = tops[span, :]
        total = functools.reduce(
            jnp.add, [jnp.exp2(logits[span, tile] - top) for tile in lane_tiles(columns)]
        )
        sums[span, :] = total
    top = tops[...].T
    total = sums[...].T
    peak = jnp.max(top, axis=0, keepdims=True)
    mass = jnp.sum(total * jnp.exp2(top - peak), axis=0, keepdims=True)
    out_ref[...] = peak + jnp.log2(mass)


def second_kernel(scale, points, x_ref, phi_ref, y_ref, e_ref, r_ref, peak_ref, left, right, part_r):
    dims, cells = x_ref.shape
    columns = y_ref.shape[1]
    block = min(512, columns)
    wide = x_ref[...] * (2.0 * scale)
    left[...] = jnp.concatenate([*pieces(wide), pad_rows(pieces(phi_ref[...]), 3)], axis=0).T
    ones = ones_rows(columns)
    y = y_ref[...]
    right[...] = jnp.concatenate([y, y, y, ones], axis=0)
    for start in range(0, columns, block):
        span = slice(start, start + block)
        part = jnp.dot(left[...], right[:, span], preferred_element_type=jnp.float32)
        e_ref[:, span] = part
        peak = jnp.max(part, axis=0, keepdims=True)
        peak_ref[:, span] = peak
        expo = jnp.exp2(e_ref[:, span] - peak)
        e_ref[:, span] = expo
        total = jnp.sum(expo, axis=0, keepdims=True)
        weight = 1.0 / (points * total)
        share = e_ref[:, span] * weight
        row = functools.reduce(jnp.add, [share[:, tile] for tile in lane_tiles(block)])
        part_r[...] = row if start == 0 else part_r[...] + row
    r_ref[...] = jnp.sum(part_r[...].T, axis=0, keepdims=True)


def third_kernel(x_ref, w_ref, e_ref, out_ref, d_ref, tall):
    dims, cells = x_ref.shape
    columns = e_ref.shape[1]
    block = min(512, columns)
    rows = lax.broadcasted_iota(jnp.int32, (16, cells), 0)
    ones = jnp.where(rows == 0, 1.0, 0.0).astype(jnp.bfloat16)
    x = jnp.concatenate([x_ref[...].astype(jnp.bfloat16), ones], axis=0)
    tall[...] = jnp.broadcast_to(w_ref[...], (LANES, cells)).T
    for start in range(0, columns, block):
        parts = []
        for at in range(start, start + block, LANES):
            q = e_ref[:, at : at + LANES] * tall[...]
            parts.append(q)
        q = jnp.concatenate(parts, axis=1)
        high = q.astype(jnp.bfloat16)
        low = (q - high.astype(jnp.float32)).astype(jnp.bfloat16)
        moved = jnp.dot(x, high, preferred_element_type=jnp.float32)
        moved = moved + jnp.dot(x, low, preferred_element_type=jnp.float32)
        total = moved[dims : dims + 1, :]
        d_ref[:, start : start + block] = total
        out_ref[:, start : start + block] = moved[:dims, :] / total


def exchange(value, axis, size, key):
    return lax.ppermute(value, axis, [(at, at ^ key) for at in range(size)])


def partners(value, axis):
    size = lax.axis_size(axis)
    if size & (size - 1) == 0 and size <= 8:
        return [exchange(value, axis, size, key) for key in range(1, size)]
    return [
        lax.ppermute(value, axis, [(at, (at + key) % size) for at in range(size)])
        for key in range(1, size)
    ]


def shards(cells, support):
    own = cells[0]
    dims, rows = own.shape
    columns = support.shape[1]
    row_size = lax.axis_size("row")
    atlases = lax.axis_size("atlas")
    total_cells = rows * row_size
    total_support = columns * lax.axis_size("col")
    share = columns // row_size
    scale = LOG2E / (blur * dims)
    row_at = lax.axis_index("row")
    atlas_at = lax.axis_index("atlas")
    paired = row_size == 2

    def gather_rows(value):
        if paired:
            return jnp.concatenate([value, exchange(value, "row", 2, 1)], axis=-1)
        return lax.all_gather(value, "row", axis=value.ndim - 1, tiled=True)

    def sum_rows(value):
        if paired:
            other = exchange(value, "row", 2, 1)
            return value + jnp.concatenate([other[:, rows:], other[:, :rows]], axis=1)
        return lax.psum(value, "row")

    def own_rows(value):
        if paired:
            return value[:, :rows]
        return lax.dynamic_slice_in_dim(value, row_at * rows, rows, 1)

    everyone = gather_rows(own.astype(jnp.float32))
    mine = lax.dynamic_slice_in_dim(support, row_at * share, share, 1)
    depth = 3 * dims + 16

    lam = pl.pallas_call(
        functools.partial(first_kernel, scale),
        out_shape=jax.ShapeDtypeStruct((1, rows), jnp.float32),
        in_specs=[VMEM, VMEM],
        out_specs=VMEM,
        scratch_shapes=[
            pltpu.VMEM((rows, depth), jnp.bfloat16),
            pltpu.VMEM((depth, columns), jnp.bfloat16),
            pltpu.VMEM((rows, columns), jnp.float32),
            pltpu.VMEM((rows, LANES), jnp.float32),
            pltpu.VMEM((rows, LANES), jnp.float32),
        ],
        compiler_params=pltpu.CompilerParams(vmem_limit_bytes=24 << 20),
        name="first",
    )(own, support)

    others = partners(lam, "col")
    peak = functools.reduce(jnp.maximum, others, lam)
    mass = functools.reduce(jnp.add, [jnp.exp2(one - peak) for one in [lam, *others]])
    phi = -math.log2(total_cells) - (peak + jnp.log2(mass))

    e, r, tops = pl.pallas_call(
        functools.partial(second_kernel, scale, float(total_support)),
        out_shape=(
            jax.ShapeDtypeStruct((total_cells, share), jnp.float32),
            jax.ShapeDtypeStruct((1, total_cells), jnp.float32),
            jax.ShapeDtypeStruct((1, share), jnp.float32),
        ),
        in_specs=[VMEM, VMEM, VMEM],
        out_specs=(VMEM, VMEM, VMEM),
        scratch_shapes=[
            pltpu.VMEM((total_cells, depth), jnp.bfloat16),
            pltpu.VMEM((depth, share), jnp.bfloat16),
            pltpu.VMEM((total_cells, LANES), jnp.float32),
        ],
        compiler_params=pltpu.CompilerParams(vmem_limit_bytes=32 << 20),
        name="second",
    )(everyone, gather_rows(phi), mine)

    r = sum_rows(r)
    r = functools.reduce(jnp.add, partners(r, "col"), r) * total_cells
    far = jnp.sum(jnp.square(own.astype(jnp.float32)), axis=0)[None, :]
    cell_dual = (blur / LOG2E) * (phi + scale * far - jnp.log2(own_rows(r)))

    moved, mass = pl.pallas_call(
        third_kernel,
        out_shape=(
            jax.ShapeDtypeStruct((dims, share), jnp.float32),
            jax.ShapeDtypeStruct((1, share), jnp.float32),
        ),
        in_specs=[VMEM, VMEM, VMEM],
        out_specs=(VMEM, VMEM),
        scratch_shapes=[pltpu.VMEM((total_cells, LANES), jnp.float32)],
        compiler_params=pltpu.CompilerParams(vmem_limit_bytes=24 << 20),
        name="third",
    )(everyone, 1.0 / r, e)

    near = jnp.sum(jnp.square(mine.astype(jnp.float32)), axis=0)[None, :]
    dual_g = (blur / LOG2E) * (scale * near - math.log2(total_support) - tops - jnp.log2(mass))

    piece = share // atlases
    if atlases & (atlases - 1) == 0 and atlases <= 8 and piece % LANES == 0:
        def slab(key):
            return lax.dynamic_slice_in_dim(moved, (atlas_at ^ key) * piece, piece, 1)

        sums = slab(0)
        arrived = [exchange(slab(key), "atlas", atlases, key) for key in range(1, atlases)]
        sums = functools.reduce(jnp.add, arrived, sums) * (1.0 / atlases)
        gathered = [sums, *partners(sums, "atlas")]

        def slot(at):
            chosen = gathered[0]
            for key in range(1, atlases):
                chosen = jnp.where(atlas_at ^ key == at, gathered[key], chosen)
            return chosen

        updated = jnp.concatenate([slot(at) for at in range(atlases)], axis=1)
    else:
        updated = lax.psum(moved, "atlas") * (1.0 / atlases)

    def in_order(value):
        if paired:
            other = exchange(value, "row", 2, 1)
            first = jnp.where(row_at == 0, value, other)
            last = jnp.where(row_at == 0, other, value)
            return jnp.concatenate([first, last], axis=1)
        return lax.all_gather(value, "row", axis=1, tiled=True)

    return (cell_dual, in_order(dual_g), in_order(updated))


def solution(mesh):
    in_specs = (P("atlas", None, "row"), P(None, "col"))
    out_specs = (P("atlas", "row"), P("atlas", "col"), P(None, "col"))
    return jax.shard_map(shards, mesh=mesh, in_specs=in_specs, out_specs=out_specs, check_vma=False)
```

```python
import functools
import math

import jax
import jax.numpy as jnp
from jax import lax
from jax.experimental import pallas as pl
from jax.experimental.pallas import tpu as pltpu
from jax.sharding import PartitionSpec as P


ITERS = 2
blur = 0.1
LANES = 128
SUBLANES = 8
LOG2E = 1.4426950408889634
VMEM = pl.BlockSpec(memory_space=pltpu.VMEM)


def pieces(value):
    high = value.astype(jnp.bfloat16)
    rest = value - high.astype(jnp.float32)
    mid = rest.astype(jnp.bfloat16)
    low = (rest - mid.astype(jnp.float32)).astype(jnp.bfloat16)
    return high, mid, low


def pad_rows(rows):
    width = rows[0].shape[1]
    index = lax.broadcasted_iota(jnp.int32, (16, width), 0)
    block = jnp.zeros((16, width), jnp.float32)
    for at, row in enumerate(rows):
        block = jnp.where(index == at, row.astype(jnp.float32), block)
    return block.astype(jnp.bfloat16)


def ones_rows(width):
    index = lax.broadcasted_iota(jnp.int32, (16, width), 0)
    return jnp.where(index < 3, 1.0, 0.0).astype(jnp.bfloat16)


def lane_tiles(width):
    return [slice(at, at + LANES) for at in range(0, width, LANES)]


def first_kernel(scale, x_ref, y_ref, out_ref, far_ref, left, right, logits, tops, sums):
    dims, rows = x_ref.shape
    columns = y_ref.shape[1]
    block = min(512, columns)
    x = x_ref[...].astype(jnp.float32)
    far_ref[...] = scale * jnp.sum(jnp.square(x), axis=0, keepdims=True)
    left[...] = jnp.concatenate([*pieces(x * (2.0 * scale)), ones_rows(rows)], axis=0).T
    for start in range(0, columns, block):
        piece = y_ref[:, start : start + block]
        near = jnp.sum(jnp.square(piece.astype(jnp.float32)), axis=0, keepdims=True)
        right[:, start : start + block] = jnp.concatenate(
            [piece, piece, piece, pad_rows(pieces(-scale * near))], axis=0
        )
    for start in range(0, columns, block):
        part = jnp.dot(
            left[...], right[:, start : start + block], preferred_element_type=jnp.float32
        )
        logits[:, start : start + block] = part
        top = functools.reduce(jnp.maximum, [part[:, tile] for tile in lane_tiles(block)])
        tops[...] = top if start == 0 else jnp.maximum(tops[...], top)
    height = min(64, rows)
    for low in range(0, rows, height):
        span = slice(low, low + height)
        top = tops[span, :]
        total = functools.reduce(
            jnp.add, [jnp.exp2(logits[span, tile] - top) for tile in lane_tiles(columns)]
        )
        sums[span, :] = total
    top = tops[...].T
    total = sums[...].T
    peak = jnp.max(top, axis=0, keepdims=True)
    mass = jnp.sum(total * jnp.exp2(top - peak), axis=0, keepdims=True)
    out_ref[...] = peak + jnp.log2(mass)


def second_kernel(scale, points, x_ref, phi_ref, y_ref, e_ref, r_ref, base_ref, left, right, part_r):
    dims, cells = x_ref.shape
    columns = y_ref.shape[1]
    block = min(512, columns)
    wide = x_ref[...] * (2.0 * scale)
    left[...] = jnp.concatenate([*pieces(wide), pad_rows(pieces(phi_ref[...]))], axis=0).T
    y = y_ref[...]
    right[...] = jnp.concatenate([y, y, y, ones_rows(columns)], axis=0)
    near = jnp.sum(jnp.square(y.astype(jnp.float32)), axis=0, keepdims=True)
    base_ref[...] = scale * near - math.log2(points)
    for start in range(0, columns, block):
        span = slice(start, start + block)
        part = jnp.dot(left[...], right[:, span], preferred_element_type=jnp.float32)
        e_ref[:, span] = part
        peak = jnp.max(part, axis=0, keepdims=True)
        base_ref[:, span] = base_ref[:, span] - peak
        expo = jnp.exp2(e_ref[:, span] - peak)
        e_ref[:, span] = expo
        total = jnp.sum(expo, axis=0, keepdims=True)
        weight = 1.0 / (points * total)
        share = e_ref[:, span] * weight
        row = functools.reduce(jnp.add, [share[:, tile] for tile in lane_tiles(block)])
        part_r[...] = row if start == 0 else part_r[...] + row
    r_ref[...] = jnp.sum(part_r[...].T, axis=0, keepdims=True)


def meet_kernel(own_ref, other_ref, out_ref):
    rows = own_ref.shape[1] // 2
    out_ref[:, :rows] = own_ref[:, :rows] + other_ref[:, rows:]
    out_ref[:, rows:] = own_ref[:, rows:] + other_ref[:, :rows]


def third_kernel(key, count, x_ref, e_ref, base_ref, *refs):
    *r_refs, out_ref, g_ref, tall = refs
    dims, cells = x_ref.shape
    width = out_ref.shape[1]
    start = 0
    if key is not None:
        start = pl.multiple_of((lax.axis_index("atlas") ^ key) * width, LANES)
    rows = lax.broadcasted_iota(jnp.int32, (16, cells), 0)
    ones = jnp.where(rows == 0, 1.0, 0.0).astype(jnp.bfloat16)
    x = jnp.concatenate([x_ref[...].astype(jnp.bfloat16), ones], axis=0)
    total = functools.reduce(jnp.add, [ref[...] for ref in r_refs])
    tall[...] = jnp.broadcast_to(1.0 / (count * total), (LANES, cells)).T
    q = e_ref[:, pl.ds(start, width)] * jnp.concatenate([tall[...]] * (width // LANES), axis=1)
    high = q.astype(jnp.bfloat16)
    low = (q - high.astype(jnp.float32)).astype(jnp.bfloat16)
    moved = jnp.dot(x, high, preferred_element_type=jnp.float32)
    moved = moved + jnp.dot(x, low, preferred_element_type=jnp.float32)
    mass = moved[dims : dims + 1, :]
    out_ref[...] = moved[:dims, :] / mass
    g_ref[...] = (blur / LOG2E) * (base_ref[:, pl.ds(start, width)] - jnp.log2(mass))


def assemble_kernel(atlases, *refs):
    own, other, g_own, g_other = refs[:atlases], refs[atlases : 2 * atlases], *refs[2 * atlases : 2 * atlases + 2]
    out_ref, g_ref, sems = refs[2 * atlases + 2 :]
    width = own[0].shape[1]
    atlas = lax.axis_index("atlas")
    row = lax.axis_index("row")
    copies = []
    for half, slabs, duals in ((row, own, g_own), (1 - row, other, g_other)):
        for key in range(atlases):
            start = pl.multiple_of((half * atlases + (atlas ^ key)) * width, LANES)
            copies.append(
                pltpu.make_async_copy(
                    slabs[key], out_ref.at[:, pl.ds(start, width)], sems.at[len(copies)]
                )
            )
            copies[-1].start()
            g_ref[:, pl.ds(start, width)] = duals[:, key * width : (key + 1) * width]
    for copy in copies:
        copy.wait()


def exchange(value, axis, size, key):
    return lax.ppermute(value, axis, [(at, at ^ key) for at in range(size)])


def partners(value, axis):
    size = lax.axis_size(axis)
    if size & (size - 1) == 0 and size <= 8:
        return [exchange(value, axis, size, key) for key in range(1, size)]
    return [
        lax.ppermute(value, axis, [(at, (at + key) % size) for at in range(size)])
        for key in range(1, size)
    ]


def shards(cells, support):
    own = cells[0]
    dims, rows = own.shape
    columns = support.shape[1]
    row_size = lax.axis_size("row")
    atlases = lax.axis_size("atlas")
    total_cells = rows * row_size
    total_support = columns * lax.axis_size("col")
    share = columns // row_size
    scale = LOG2E / (blur * dims)
    row_at = lax.axis_index("row")
    paired = row_size == 2

    def gather_rows(value):
        if paired:
            return jnp.concatenate([value, exchange(value, "row", 2, 1)], axis=-1)
        return lax.all_gather(value, "row", axis=value.ndim - 1, tiled=True)

    def sum_rows(value):
        if paired:
            return pl.pallas_call(
                meet_kernel,
                out_shape=jax.ShapeDtypeStruct(value.shape, jnp.float32),
                in_specs=[VMEM, VMEM],
                out_specs=VMEM,
                compiler_params=pltpu.CompilerParams(vmem_limit_bytes=4 << 20),
                name="meet",
            )(value, exchange(value, "row", 2, 1))
        return lax.psum(value, "row")

    def own_rows(value):
        if paired:
            return value[:, :rows]
        return lax.dynamic_slice_in_dim(value, row_at * rows, rows, 1)

    def all_rows(value):
        return lax.all_gather(value, "row", axis=1, tiled=True)

    everyone = gather_rows(own.astype(jnp.float32))
    mine = lax.dynamic_slice_in_dim(support, row_at * share, share, 1)
    depth = 3 * dims + 16

    def row_vector(width):
        return jax.ShapeDtypeStruct((1, width), jnp.float32)

    lam, far = pl.pallas_call(
        functools.partial(first_kernel, scale),
        out_shape=(row_vector(rows), row_vector(rows)),
        in_specs=[VMEM, VMEM],
        out_specs=(VMEM, VMEM),
        scratch_shapes=[
            pltpu.VMEM((rows, depth), jnp.bfloat16),
            pltpu.VMEM((depth, columns), jnp.bfloat16),
            pltpu.VMEM((rows, columns), jnp.float32),
            pltpu.VMEM((rows, LANES), jnp.float32),
            pltpu.VMEM((rows, LANES), jnp.float32),
        ],
        compiler_params=pltpu.CompilerParams(vmem_limit_bytes=24 << 20),
        name="first",
    )(own, support)

    others = partners(lam, "col")
    peak = functools.reduce(jnp.maximum, others, lam)
    mass = functools.reduce(jnp.add, [jnp.exp2(one - peak) for one in [lam, *others]])
    phi = -math.log2(total_cells) - (peak + jnp.log2(mass))

    e, r, base = pl.pallas_call(
        functools.partial(second_kernel, scale, float(total_support)),
        out_shape=(
            jax.ShapeDtypeStruct((total_cells, share), jnp.float32),
            row_vector(total_cells),
            row_vector(share),
        ),
        in_specs=[VMEM, VMEM, VMEM],
        out_specs=(VMEM, VMEM, VMEM),
        scratch_shapes=[
            pltpu.VMEM((total_cells, depth), jnp.bfloat16),
            pltpu.VMEM((depth, share), jnp.bfloat16),
            pltpu.VMEM((total_cells, LANES), jnp.float32),
        ],
        compiler_params=pltpu.CompilerParams(vmem_limit_bytes=32 << 20),
        name="second",
    )(everyone, gather_rows(phi), mine)

    r = sum_rows(r)
    shares = [r, *partners(r, "col")]

    def third(key, width):
        return pl.pallas_call(
            functools.partial(third_kernel, key, float(total_cells)),
            out_shape=(jax.ShapeDtypeStruct((dims, width), jnp.float32), row_vector(width)),
            in_specs=[VMEM] * (3 + len(shares)),
            out_specs=(VMEM, VMEM),
            scratch_shapes=[pltpu.VMEM((total_cells, LANES), jnp.float32)],
            compiler_params=pltpu.CompilerParams(vmem_limit_bytes=24 << 20),
            name="third",
        )(everyone, e, base, *shares)

    piece = share // atlases
    if paired and atlases & (atlases - 1) == 0 and atlases <= 8 and piece % LANES == 0:

        order = sorted(range(atlases), key=lambda key: (key == 0, -key))
        terms, duals, arrived = [None] * atlases, [None] * atlases, []
        for key in order:
            terms[key], duals[key] = third(key, piece)
            if key:
                arrived.append(exchange(terms[key], "atlas", atlases, key))
        sums = functools.reduce(jnp.add, arrived, terms[0]) * (1.0 / atlases)
        slabs = [sums, *partners(sums, "atlas")]
        duals = jnp.concatenate(duals, axis=1)
        updated, dual_g = pl.pallas_call(
            functools.partial(assemble_kernel, atlases),
            out_shape=(jax.ShapeDtypeStruct((dims, columns), jnp.float32), row_vector(columns)),
            in_specs=[VMEM] * (2 * atlases + 2),
            out_specs=(pl.BlockSpec(memory_space=pl.ANY), VMEM),
            scratch_shapes=[pltpu.SemaphoreType.DMA((2 * atlases,))],
            compiler_params=pltpu.CompilerParams(vmem_limit_bytes=8 << 20),
            name="assemble",
        )(
            *slabs,
            *[exchange(slab, "row", 2, 1) for slab in slabs],
            duals,
            exchange(duals, "row", 2, 1),
        )
    else:
        moved, dual_g = third(None, share)
        updated = all_rows(lax.psum(moved, "atlas") * (1.0 / atlases))
        dual_g = all_rows(dual_g)

    cell_dual = (blur / LOG2E) * (
        phi + far - jnp.log2(total_cells * own_rows(functools.reduce(jnp.add, shares)))
    )

    return (cell_dual, dual_g, updated)


def solution(mesh):
    in_specs = (P("atlas", None, "row"), P(None, "col"))
    out_specs = (P("atlas", "row"), P("atlas", "col"), P(None, "col"))
    return jax.shard_map(shards, mesh=mesh, in_specs=in_specs, out_specs=out_specs, check_vma=False)
```

```python
import functools
import math

import jax
import jax.numpy as jnp
from jax import lax
from jax.experimental import pallas as pl
from jax.experimental.pallas import tpu as pltpu
from jax.sharding import PartitionSpec as P


blur = 0.1
LANES = 128
SUBLANES = 8
LOG2E = 1.4426950408889634
VMEM = pl.BlockSpec(memory_space=pltpu.VMEM)
HBM = pl.BlockSpec(memory_space=pltpu.HBM)


def pieces(value):
    high = value.astype(jnp.bfloat16)
    rest = value - high.astype(jnp.float32)
    mid = rest.astype(jnp.bfloat16)
    low = (rest - mid.astype(jnp.float32)).astype(jnp.bfloat16)
    return high, mid, low


def pad_rows(rows):
    width = rows[0].shape[1]
    index = lax.broadcasted_iota(jnp.int32, (16, width), 0)
    block = jnp.zeros((16, width), jnp.float32)
    for at, row in enumerate(rows):
        block = jnp.where(index == at, row.astype(jnp.float32), block)
    return block.astype(jnp.bfloat16)


def ones_rows(width):
    index = lax.broadcasted_iota(jnp.int32, (16, width), 0)
    return jnp.where(index < 3, 1.0, 0.0).astype(jnp.bfloat16)


def lane_tiles(width):
    return [slice(at, at + LANES) for at in range(0, width, LANES)]


def first_kernel(
    scale, x_hbm, y_hbm, out_ref, far_ref, x_ref, y_ref, left, right, logits, tops, sums, sems
):
    _, rows = x_ref.shape
    columns = y_ref.shape[1]
    block = min(512, columns)
    starts = range(0, columns, block)
    copies = [pltpu.make_async_copy(x_hbm, x_ref, sems.at[0])]
    for at, start in enumerate(starts):
        span = slice(start, start + block)
        copies.append(pltpu.make_async_copy(y_hbm.at[:, span], y_ref.at[:, span], sems.at[1 + at]))
    for copy in copies:
        copy.start()
    copies[0].wait()
    x = x_ref[...]
    far_ref[...] = scale * jnp.sum(jnp.square(x.astype(jnp.float32)), axis=0, keepdims=True)
    left[...] = jnp.concatenate([x, ones_rows(rows)], axis=0).T
    for at, start in enumerate(starts):
        span = slice(start, start + block)
        copies[1 + at].wait()
        piece = y_ref[:, span]
        near = jnp.sum(jnp.square(piece.astype(jnp.float32)), axis=0, keepdims=True)
        right[:, span] = jnp.concatenate([piece, pad_rows(pieces(-0.5 * near))], axis=0)
        part = jnp.dot(left[...], right[:, span], preferred_element_type=jnp.float32)
        part = part * (2.0 * scale)
        logits[:, span] = part
        top = functools.reduce(jnp.maximum, [part[:, tile] for tile in lane_tiles(block)])
        tops[...] = top if start == 0 else jnp.maximum(tops[...], top)
    height = min(64, rows)
    for low in range(0, rows, height):
        span = slice(low, low + height)
        top = tops[span, :]
        total = functools.reduce(
            jnp.add, [jnp.exp2(logits[span, tile] - top) for tile in lane_tiles(columns)]
        )
        sums[span, :] = total
    top = tops[...].T
    total = sums[...].T
    peak = jnp.max(top, axis=0, keepdims=True)
    mass = jnp.sum(total * jnp.exp2(top - peak), axis=0, keepdims=True)
    out_ref[...] = peak + jnp.log2(mass)


def second_kernel(scale, points, x_ref, phi_ref, y_ref, e_ref, r_ref, base_ref, left, right, part_r):
    columns = y_ref.shape[1]
    block = min(512, columns)
    shift = pad_rows(pieces(phi_ref[...] * (0.5 / scale)))
    left[...] = jnp.concatenate([x_ref[...].astype(jnp.bfloat16), shift], axis=0).T
    y = y_ref[...]
    right[...] = jnp.concatenate([y, ones_rows(columns)], axis=0)
    near = jnp.sum(jnp.square(y.astype(jnp.float32)), axis=0, keepdims=True)
    base_ref[...] = scale * near - math.log2(points)
    for start in range(0, columns, block):
        span = slice(start, start + block)
        part = jnp.dot(left[...], right[:, span], preferred_element_type=jnp.float32)
        part = part * (2.0 * scale)
        e_ref[:, span] = part
        peak = jnp.max(part, axis=0, keepdims=True)
        base_ref[:, span] = base_ref[:, span] - peak
        expo = jnp.exp2(e_ref[:, span] - peak)
        e_ref[:, span] = expo
        total = jnp.sum(expo, axis=0, keepdims=True)
        weight = 1.0 / (points * total)
        share = e_ref[:, span] * weight
        row = functools.reduce(jnp.add, [share[:, tile] for tile in lane_tiles(block)])
        part_r[...] = row if start == 0 else part_r[...] + row
    r_ref[...] = jnp.sum(part_r[...].T, axis=0, keepdims=True)


def meet_kernel(own_ref, other_ref, out_ref):
    rows = own_ref.shape[1] // 2
    out_ref[:, :rows] = own_ref[:, :rows] + other_ref[:, rows:]
    out_ref[:, rows:] = own_ref[:, rows:] + other_ref[:, :rows]


def split_kernel(e_ref, after_ref, high_ref, low_ref):
    del after_ref
    for tile in lane_tiles(e_ref.shape[1]):
        e = e_ref[:, tile]
        high = e.astype(jnp.bfloat16)
        high_ref[:, tile] = high
        low_ref[:, tile] = (e - high.astype(jnp.float32)).astype(jnp.bfloat16)


def weights_kernel(count, x_ref, *refs):
    *r_refs, out_ref = refs
    w = 1.0 / (count * functools.reduce(jnp.add, [ref[...] for ref in r_refs]))
    wide = x_ref[...] * w
    high = wide.astype(jnp.bfloat16)
    low = (wide - high.astype(jnp.float32)).astype(jnp.bfloat16)
    out_ref[...] = jnp.concatenate([high, pad_rows(pieces(w)), low], axis=0)


def third_kernel(key, dims, weights_ref, high_ref, low_ref, base_ref, out_ref, g_ref):
    width = out_ref.shape[1]
    start = 0
    if key is not None:
        start = pl.multiple_of((lax.axis_index("atlas") ^ key) * width, LANES)
    span = pl.ds(start, width)
    upper = dims + 16
    moved = jnp.dot(weights_ref[...], high_ref[:, span], preferred_element_type=jnp.float32)
    rest = jnp.dot(weights_ref[:upper, :], low_ref[:, span], preferred_element_type=jnp.float32)
    mass = jnp.sum(moved[dims:upper, :] + rest[dims:upper, :], axis=0, keepdims=True)
    out_ref[...] = (moved[:dims, :] + moved[upper:, :] + rest[:dims, :]) / mass
    g_ref[...] = (blur / LOG2E) * (base_ref[:, span] - jnp.log2(mass))


def assemble_kernel(atlases, *refs):
    own, other, g_own, g_other = refs[:atlases], refs[atlases : 2 * atlases], *refs[2 * atlases : 2 * atlases + 2]
    out_ref, g_ref, image, sems = refs[2 * atlases + 2 :]
    dims, width = own[0].shape
    atlas = lax.axis_index("atlas")
    row = lax.axis_index("row")
    places = []
    for half, slabs, duals in ((row, own, g_own), (1 - row, other, g_other)):
        for key in range(atlases):
            start = pl.multiple_of((half * atlases + (atlas ^ key)) * width, LANES)
            places.append((slabs[key], start))
            g_ref[:, pl.ds(start, width)] = duals[:, key * width : (key + 1) * width]
    copies = []
    for low in range(0, dims, SUBLANES):
        rows = slice(low, low + SUBLANES)
        for slab, start in places:
            image[rows, pl.ds(start, width)] = slab[rows, :]
        copies.append(
            pltpu.make_async_copy(image.at[rows, :], out_ref.at[rows, :], sems.at[len(copies)])
        )
        copies[-1].start()
    for copy in copies:
        copy.wait()


def exchange(value, axis, size, key):
    return lax.ppermute(value, axis, [(at, at ^ key) for at in range(size)])


def partners(value, axis):
    size = lax.axis_size(axis)
    if size & (size - 1) == 0 and size <= 8:
        return [exchange(value, axis, size, key) for key in range(1, size)]
    return [
        lax.ppermute(value, axis, [(at, (at + key) % size) for at in range(size)])
        for key in range(1, size)
    ]


def shards(cells, support):
    own = cells[0]
    dims, rows = own.shape
    columns = support.shape[1]
    row_size = lax.axis_size("row")
    atlases = lax.axis_size("atlas")
    total_cells = rows * row_size
    total_support = columns * lax.axis_size("col")
    share = columns // row_size
    scale = LOG2E / (blur * dims)
    row_at = lax.axis_index("row")
    paired = row_size == 2

    def gather_rows(value):
        if paired:
            return jnp.concatenate([value, exchange(value, "row", 2, 1)], axis=-1)
        return lax.all_gather(value, "row", axis=value.ndim - 1, tiled=True)

    def sum_rows(value):
        if paired:
            return pl.pallas_call(
                meet_kernel,
                out_shape=jax.ShapeDtypeStruct(value.shape, jnp.float32),
                in_specs=[VMEM, VMEM],
                out_specs=VMEM,
                compiler_params=pltpu.CompilerParams(vmem_limit_bytes=4 << 20),
                name="meet",
            )(value, exchange(value, "row", 2, 1))
        return lax.psum(value, "row")

    def own_rows(value):
        if paired:
            return value[:, :rows]
        return lax.dynamic_slice_in_dim(value, row_at * rows, rows, 1)

    def all_rows(value):
        return lax.all_gather(value, "row", axis=1, tiled=True)

    everyone = gather_rows(own.astype(jnp.float32))
    mine = lax.dynamic_slice_in_dim(support, row_at * share, share, 1)
    depth = dims + 16

    def row_vector(width):
        return jax.ShapeDtypeStruct((1, width), jnp.float32)

    lam, far = pl.pallas_call(
        functools.partial(first_kernel, scale),
        out_shape=(row_vector(rows), row_vector(rows)),
        in_specs=[HBM, HBM],
        out_specs=(VMEM, VMEM),
        scratch_shapes=[
            pltpu.VMEM((dims, rows), jnp.bfloat16),
            pltpu.VMEM((dims, columns), jnp.bfloat16),
            pltpu.VMEM((rows, depth), jnp.bfloat16),
            pltpu.VMEM((depth, columns), jnp.bfloat16),
            pltpu.VMEM((rows, columns), jnp.float32),
            pltpu.VMEM((rows, LANES), jnp.float32),
            pltpu.VMEM((rows, LANES), jnp.float32),
            pltpu.SemaphoreType.DMA((1 + columns // min(512, columns),)),
        ],
        compiler_params=pltpu.CompilerParams(vmem_limit_bytes=56_510_000),
        name="first",
    )(own, support)

    others = partners(lam, "col")
    peak = functools.reduce(jnp.maximum, others, lam)
    mass = functools.reduce(jnp.add, [jnp.exp2(one - peak) for one in [lam, *others]])
    phi = -math.log2(total_cells) - (peak + jnp.log2(mass))

    e, r, base = pl.pallas_call(
        functools.partial(second_kernel, scale, float(total_support)),
        out_shape=(
            jax.ShapeDtypeStruct((total_cells, share), jnp.float32),
            row_vector(total_cells),
            row_vector(share),
        ),
        in_specs=[VMEM, VMEM, VMEM],
        out_specs=(VMEM, VMEM, VMEM),
        scratch_shapes=[
            pltpu.VMEM((total_cells, depth), jnp.bfloat16),
            pltpu.VMEM((depth, share), jnp.bfloat16),
            pltpu.VMEM((total_cells, LANES), jnp.float32),
        ],
        compiler_params=pltpu.CompilerParams(vmem_limit_bytes=32 << 20),
        name="second",
    )(everyone, gather_rows(phi), mine)

    r = sum_rows(r)
    shares = [r, *partners(r, "col")]

    high, low = pl.pallas_call(
        split_kernel,
        out_shape=(jax.ShapeDtypeStruct(e.shape, jnp.bfloat16),) * 2,
        in_specs=[VMEM, VMEM],
        out_specs=(VMEM, VMEM),
        compiler_params=pltpu.CompilerParams(vmem_limit_bytes=24 << 20),
        cost_estimate=pl.CostEstimate(flops=e.size * 4, bytes_accessed=e.size * 8, transcendentals=0),
        name="split",
    )(e, r)
    weights = pl.pallas_call(
        functools.partial(weights_kernel, float(total_cells)),
        out_shape=jax.ShapeDtypeStruct((2 * dims + 16, total_cells), jnp.bfloat16),
        in_specs=[VMEM] * (1 + len(shares)),
        out_specs=VMEM,
        compiler_params=pltpu.CompilerParams(vmem_limit_bytes=16 << 20),
        name="weights",
    )(everyone, *shares)

    def third(key, width):
        return pl.pallas_call(
            functools.partial(third_kernel, key, dims),
            out_shape=(jax.ShapeDtypeStruct((dims, width), jnp.float32), row_vector(width)),
            in_specs=[VMEM] * 4,
            out_specs=(VMEM, VMEM),
            compiler_params=pltpu.CompilerParams(vmem_limit_bytes=16 << 20),
            cost_estimate=pl.CostEstimate(
                flops=2 * (3 * dims + 32) * total_cells * width,
                bytes_accessed=4 * total_cells * width,
                transcendentals=0,
            ),
            name="third",
        )(weights, high, low, base)

    piece = share // atlases
    if paired and atlases & (atlases - 1) == 0 and atlases <= 8 and piece % LANES == 0:

        order = [*range(1, atlases), 0]
        terms, duals, arrived = [None] * atlases, [None] * atlases, []
        for key in order:
            terms[key], duals[key] = third(key, piece)
            if key:
                arrived.append(exchange(terms[key], "atlas", atlases, key))
        sums = functools.reduce(jnp.add, arrived, terms[0]) * (1.0 / atlases)
        slabs = [sums, *partners(sums, "atlas")]
        duals = jnp.concatenate(duals, axis=1)
        updated, dual_g = pl.pallas_call(
            functools.partial(assemble_kernel, atlases),
            out_shape=(jax.ShapeDtypeStruct((dims, columns), jnp.float32), row_vector(columns)),
            in_specs=[VMEM] * (2 * atlases + 2),
            out_specs=(HBM, VMEM),
            scratch_shapes=[
                pltpu.VMEM((dims, columns), jnp.float32),
                pltpu.SemaphoreType.DMA((dims // SUBLANES,)),
            ],
            compiler_params=pltpu.CompilerParams(vmem_limit_bytes=8 << 20),
            name="assemble",
        )(
            *slabs,
            *[exchange(slab, "row", 2, 1) for slab in slabs],
            duals,
            exchange(duals, "row", 2, 1),
        )
    else:
        moved, dual_g = third(None, share)
        updated = all_rows(lax.psum(moved, "atlas") * (1.0 / atlases))
        dual_g = all_rows(dual_g)

    cell_dual = (blur / LOG2E) * (
        phi + far - jnp.log2(total_cells * own_rows(functools.reduce(jnp.add, shares)))
    )

    return (cell_dual, dual_g, updated)


def solution(mesh):
    in_specs = (P("atlas", None, "row"), P(None, "col"))
    out_specs = (P("atlas", "row"), P("atlas", "col"), P(None, "col"))
    return jax.shard_map(shards, mesh=mesh, in_specs=in_specs, out_specs=out_specs, check_vma=False)
```

```python
import functools
import math

import jax
import jax.numpy as jnp
from jax import lax
from jax.experimental import pallas as pl
from jax.experimental.pallas import tpu as pltpu
from jax.sharding import PartitionSpec as P


blur = 0.1
LANES = 128
SUBLANES = 8
LOG2E = 1.4426950408889634
VMEM = pl.BlockSpec(memory_space=pltpu.VMEM)
HBM = pl.BlockSpec(memory_space=pltpu.HBM)


def pieces(value):
    high = value.astype(jnp.bfloat16)
    rest = value - high.astype(jnp.float32)
    mid = rest.astype(jnp.bfloat16)
    low = (rest - mid.astype(jnp.float32)).astype(jnp.bfloat16)
    return high, mid, low


def pad_rows(rows):
    width = rows[0].shape[1]
    index = lax.broadcasted_iota(jnp.int32, (16, width), 0)
    block = jnp.zeros((16, width), jnp.float32)
    for at, row in enumerate(rows):
        block = jnp.where(index == at, row.astype(jnp.float32), block)
    return block.astype(jnp.bfloat16)


def ones_rows(width):
    index = lax.broadcasted_iota(jnp.int32, (16, width), 0)
    return jnp.where(index < 3, 1.0, 0.0).astype(jnp.bfloat16)


def lane_tiles(width):
    return [slice(at, at + LANES) for at in range(0, width, LANES)]


def first_kernel(
    scale, x_hbm, y_hbm, out_ref, far_ref, x_ref, y_ref, left, right, logits, tops, sums, sems
):
    _, rows = x_ref.shape
    columns = y_ref.shape[1]
    block = min(512, columns)
    starts = range(0, columns, block)
    first_copy = pltpu.make_async_copy(x_hbm, x_ref, sems.at[0])
    first_copy.start()
    waits = {}
    count = sems.shape[0] - 1
    for at in range(count):
        span = slice(at * columns // count, (at + 1) * columns // count)
        waits[at * len(starts) // count] = pltpu.make_async_copy(
            y_hbm.at[:, span], y_ref.at[:, span], sems.at[1 + at]
        )
    for copy in waits.values():
        copy.start()
    first_copy.wait()
    x = x_ref[...]
    far_ref[...] = scale * jnp.sum(jnp.square(x.astype(jnp.float32)), axis=0, keepdims=True)
    wide = x.astype(jnp.float32) * (2.0 * scale)
    left[...] = jnp.concatenate([*pieces(wide), ones_rows(rows)], axis=0).T
    for at, start in enumerate(starts):
        span = slice(start, start + block)
        if at in waits:
            waits[at].wait()
        piece = y_ref[:, span]
        near = jnp.sum(jnp.square(piece.astype(jnp.float32)), axis=0, keepdims=True)
        right[:, span] = jnp.concatenate(
            [piece, piece, piece, pad_rows(pieces(-scale * near))], axis=0
        )
        part = jnp.dot(left[...], right[:, span], preferred_element_type=jnp.float32)
        logits[:, span] = part
        top = functools.reduce(jnp.maximum, [part[:, tile] for tile in lane_tiles(block)])
        tops[...] = top if start == 0 else jnp.maximum(tops[...], top)
    height = min(64, rows)
    for low in range(0, rows, height):
        span = slice(low, low + height)
        top = tops[span, :]
        total = functools.reduce(
            jnp.add, [jnp.exp2(logits[span, tile] - top) for tile in lane_tiles(columns)]
        )
        sums[span, :] = total
    top = tops[...].T
    total = sums[...].T
    peak = jnp.max(top, axis=0, keepdims=True)
    mass = jnp.sum(total * jnp.exp2(top - peak), axis=0, keepdims=True)
    out_ref[...] = peak + jnp.log2(mass)


def second_kernel(scale, points, x_ref, phi_ref, y_ref, e_ref, r_ref, base_ref, left, right, part_r):
    columns = y_ref.shape[1]
    block = min(512, columns)
    wide = x_ref[...] * (2.0 * scale)
    left[...] = jnp.concatenate([*pieces(wide), pad_rows(pieces(phi_ref[...]))], axis=0).T
    y = y_ref[...]
    right[...] = jnp.concatenate([y, y, y, ones_rows(columns)], axis=0)
    near = jnp.sum(jnp.square(y.astype(jnp.float32)), axis=0, keepdims=True)
    base_ref[...] = scale * near - math.log2(points)
    for start in range(0, columns, block):
        span = slice(start, start + block)
        part = jnp.dot(left[...], right[:, span], preferred_element_type=jnp.float32)
        e_ref[:, span] = part
        peak = jnp.max(part, axis=0, keepdims=True)
        base_ref[:, span] = base_ref[:, span] - peak
        expo = jnp.exp2(e_ref[:, span] - peak)
        e_ref[:, span] = expo
        total = jnp.sum(expo, axis=0, keepdims=True)
        weight = 1.0 / (points * total)
        share = e_ref[:, span] * weight
        row = functools.reduce(jnp.add, [share[:, tile] for tile in lane_tiles(block)])
        part_r[...] = row if start == 0 else part_r[...] + row
    r_ref[...] = jnp.sum(part_r[...].T, axis=0, keepdims=True)


def meet_kernel(own_ref, other_ref, out_ref):
    rows = own_ref.shape[1] // 2
    out_ref[:, :rows] = own_ref[:, :rows] + other_ref[:, rows:]
    out_ref[:, rows:] = own_ref[:, rows:] + other_ref[:, :rows]


def split_kernel(e_ref, after_ref, high_ref, low_ref):
    del after_ref
    height = min(32, e_ref.shape[0])

    @pl.loop(0, e_ref.shape[0] // height)
    def _(at):
        span = pl.ds(pl.multiple_of(at * height, height), height)
        e = e_ref[span, :]
        high = e.astype(jnp.bfloat16)
        high_ref[span, :] = high
        low_ref[span, :] = (e - high.astype(jnp.float32)).astype(jnp.bfloat16)


def weights_kernel(count, x_ref, *refs):
    *r_refs, out_ref = refs
    w = 1.0 / (count * functools.reduce(jnp.add, [ref[...] for ref in r_refs]))
    wide = x_ref[...] * w
    high = wide.astype(jnp.bfloat16)
    low = (wide - high.astype(jnp.float32)).astype(jnp.bfloat16)
    out_ref[...] = jnp.concatenate([high, pad_rows(pieces(w)), low], axis=0)


def third_kernel(key, dims, weights_ref, high_ref, low_ref, base_ref, out_ref, g_ref):
    width = out_ref.shape[1]
    start = 0
    if key is not None:
        start = pl.multiple_of((lax.axis_index("atlas") ^ key) * width, LANES)
    span = pl.ds(start, width)
    upper = dims + 16
    moved = jnp.dot(weights_ref[...], high_ref[:, span], preferred_element_type=jnp.float32)
    rest = jnp.dot(weights_ref[:upper, :], low_ref[:, span], preferred_element_type=jnp.float32)
    mass = jnp.sum(moved[dims:upper, :] + rest[dims:upper, :], axis=0, keepdims=True)
    out_ref[...] = (moved[:dims, :] + moved[upper:, :] + rest[:dims, :]) / mass
    g_ref[...] = (blur / LOG2E) * (base_ref[:, span] - jnp.log2(mass))


def assemble_kernel(atlases, *refs):
    own, other, g_own, g_other = refs[:atlases], refs[atlases : 2 * atlases], *refs[2 * atlases : 2 * atlases + 2]
    out_ref, g_hbm, image, g_ref, sems = refs[2 * atlases + 2 :]
    dims, width = own[0].shape
    atlas = lax.axis_index("atlas")
    row = lax.axis_index("row")
    places = []
    for half, slabs, duals in ((row, own, g_own), (1 - row, other, g_other)):
        for key in range(atlases):
            start = pl.multiple_of((half * atlases + (atlas ^ key)) * width, LANES)
            places.append((slabs[key], start))
            g_ref[:, pl.ds(start, width)] = duals[:, key * width : (key + 1) * width]
    copies = [pltpu.make_async_copy(g_ref, g_hbm, sems.at[0])]
    copies[0].start()
    for low in range(0, dims, SUBLANES):
        rows = slice(low, low + SUBLANES)
        for slab, start in places:
            image[rows, pl.ds(start, width)] = slab[rows, :]
        copies.append(
            pltpu.make_async_copy(image.at[rows, :], out_ref.at[rows, :], sems.at[len(copies)])
        )
        copies[-1].start()
    for copy in copies:
        copy.wait()


def exchange(value, axis, size, key):
    return lax.ppermute(value, axis, [(at, at ^ key) for at in range(size)])


def partners(value, axis):
    size = lax.axis_size(axis)
    if size & (size - 1) == 0 and size <= 8:
        return [exchange(value, axis, size, key) for key in range(1, size)]
    return [
        lax.ppermute(value, axis, [(at, (at + key) % size) for at in range(size)])
        for key in range(1, size)
    ]


def shards(cells, support):
    own = cells[0]
    dims, rows = own.shape
    columns = support.shape[1]
    row_size = lax.axis_size("row")
    atlases = lax.axis_size("atlas")
    total_cells = rows * row_size
    total_support = columns * lax.axis_size("col")
    share = columns // row_size
    scale = LOG2E / (blur * dims)
    row_at = lax.axis_index("row")
    paired = row_size == 2

    def gather_rows(value):
        if paired:
            return jnp.concatenate([value, exchange(value, "row", 2, 1)], axis=-1)
        return lax.all_gather(value, "row", axis=value.ndim - 1, tiled=True)

    def sum_rows(value):
        if paired:
            return pl.pallas_call(
                meet_kernel,
                out_shape=jax.ShapeDtypeStruct(value.shape, jnp.float32),
                in_specs=[VMEM, VMEM],
                out_specs=VMEM,
                compiler_params=pltpu.CompilerParams(vmem_limit_bytes=4 << 20),
                name="meet",
            )(value, exchange(value, "row", 2, 1))
        return lax.psum(value, "row")

    def own_rows(value):
        if paired:
            return value[:, :rows]
        return lax.dynamic_slice_in_dim(value, row_at * rows, rows, 1)

    def all_rows(value):
        return lax.all_gather(value, "row", axis=1, tiled=True)

    everyone = gather_rows(own.astype(jnp.float32))
    mine = lax.dynamic_slice_in_dim(support, row_at * share, share, 1)
    depth = 3 * dims + 16

    def row_vector(width):
        return jax.ShapeDtypeStruct((1, width), jnp.float32)

    lam, far = pl.pallas_call(
        functools.partial(first_kernel, scale),
        out_shape=(row_vector(rows), row_vector(rows)),
        in_specs=[HBM, HBM],
        out_specs=(VMEM, VMEM),
        scratch_shapes=[
            pltpu.VMEM((dims, rows), jnp.bfloat16),
            pltpu.VMEM((dims, columns), jnp.bfloat16),
            pltpu.VMEM((rows, depth), jnp.bfloat16),
            pltpu.VMEM((depth, columns), jnp.bfloat16),
            pltpu.VMEM((rows, columns), jnp.float32),
            pltpu.VMEM((rows, LANES), jnp.float32),
            pltpu.VMEM((rows, LANES), jnp.float32),
            pltpu.SemaphoreType.DMA((3 if columns % 1024 == 0 else 2,)),
        ],
        compiler_params=pltpu.CompilerParams(vmem_limit_bytes=56_510_000),
        name="first",
    )(own, support)

    others = partners(lam, "col")
    peak = functools.reduce(jnp.maximum, others, lam)
    mass = functools.reduce(jnp.add, [jnp.exp2(one - peak) for one in [lam, *others]])
    phi = -math.log2(total_cells) - (peak + jnp.log2(mass))

    e, r, base = pl.pallas_call(
        functools.partial(second_kernel, scale, float(total_support)),
        out_shape=(
            jax.ShapeDtypeStruct((total_cells, share), jnp.float32),
            row_vector(total_cells),
            row_vector(share),
        ),
        in_specs=[VMEM, VMEM, VMEM],
        out_specs=(VMEM, VMEM, VMEM),
        scratch_shapes=[
            pltpu.VMEM((total_cells, depth), jnp.bfloat16),
            pltpu.VMEM((depth, share), jnp.bfloat16),
            pltpu.VMEM((total_cells, LANES), jnp.float32),
        ],
        compiler_params=pltpu.CompilerParams(vmem_limit_bytes=32 << 20),
        name="second",
    )(everyone, gather_rows(phi), mine)

    r = sum_rows(r)
    shares = [r, *partners(r, "col")]

    high, low = pl.pallas_call(
        split_kernel,
        out_shape=(jax.ShapeDtypeStruct(e.shape, jnp.bfloat16),) * 2,
        in_specs=[VMEM, VMEM],
        out_specs=(VMEM, VMEM),
        compiler_params=pltpu.CompilerParams(vmem_limit_bytes=24 << 20),
        cost_estimate=pl.CostEstimate(flops=e.size * 4, bytes_accessed=e.size * 8, transcendentals=0),
        name="split",
    )(e, r)
    weights = pl.pallas_call(
        functools.partial(weights_kernel, float(total_cells)),
        out_shape=jax.ShapeDtypeStruct((2 * dims + 16, total_cells), jnp.bfloat16),
        in_specs=[VMEM] * (1 + len(shares)),
        out_specs=VMEM,
        compiler_params=pltpu.CompilerParams(vmem_limit_bytes=16 << 20),
        name="weights",
    )(everyone, *shares)

    def third(key, width):
        return pl.pallas_call(
            functools.partial(third_kernel, key, dims),
            out_shape=(jax.ShapeDtypeStruct((dims, width), jnp.float32), row_vector(width)),
            in_specs=[VMEM] * 4,
            out_specs=(VMEM, VMEM),
            compiler_params=pltpu.CompilerParams(vmem_limit_bytes=16 << 20),
            cost_estimate=pl.CostEstimate(
                flops=2 * (3 * dims + 32) * total_cells * width,
                bytes_accessed=4 * total_cells * width,
                transcendentals=0,
            ),
            name="third",
        )(weights, high, low, base)

    piece = share // atlases
    if paired and atlases & (atlases - 1) == 0 and atlases <= 8 and piece % LANES == 0:

        order = [*range(atlases - 1, 0, -1), 0]
        terms, duals, arrived = [None] * atlases, [None] * atlases, []
        for key in order:
            terms[key], duals[key] = third(key, piece)
            if key:
                arrived.append(exchange(terms[key], "atlas", atlases, key))
        sums = functools.reduce(jnp.add, arrived, terms[0]) * (1.0 / atlases)
        slabs = [sums, *partners(sums, "atlas")]
        duals = jnp.concatenate(duals, axis=1)
        updated, dual_g = pl.pallas_call(
            functools.partial(assemble_kernel, atlases),
            out_shape=(jax.ShapeDtypeStruct((dims, columns), jnp.float32), row_vector(columns)),
            in_specs=[VMEM] * (2 * atlases + 2),
            out_specs=(HBM, HBM),
            scratch_shapes=[
                pltpu.VMEM((dims, columns), jnp.float32),
                pltpu.VMEM((1, columns), jnp.float32),
                pltpu.SemaphoreType.DMA((1 + dims // SUBLANES,)),
            ],
            compiler_params=pltpu.CompilerParams(vmem_limit_bytes=8 << 20),
            name="assemble",
        )(
            *slabs,
            *[exchange(slab, "row", 2, 1) for slab in slabs],
            duals,
            exchange(duals, "row", 2, 1),
        )
    else:
        moved, dual_g = third(None, share)
        updated = all_rows(lax.psum(moved, "atlas") * (1.0 / atlases))
        dual_g = all_rows(dual_g)

    cell_dual = (blur / LOG2E) * (
        phi + far - jnp.log2(total_cells * own_rows(functools.reduce(jnp.add, shares)))
    )

    return (cell_dual, dual_g, updated)


def solution(mesh):
    in_specs = (P("atlas", None, "row"), P(None, "col"))
    out_specs = (P("atlas", "row"), P("atlas", "col"), P(None, "col"))
    return jax.shard_map(shards, mesh=mesh, in_specs=in_specs, out_specs=out_specs, check_vma=False)
```

```python
import functools
import math

import jax
import jax.numpy as jnp
from jax import lax
from jax.experimental import pallas as pl
from jax.experimental.pallas import tpu as pltpu
from jax.sharding import PartitionSpec as P


blur = 0.1
LANES = 128
SUBLANES = 8
LOG2E = 1.4426950408889634
VMEM = pl.BlockSpec(memory_space=pltpu.VMEM)
HBM = pl.BlockSpec(memory_space=pltpu.HBM)


def pieces(value):
    high = value.astype(jnp.bfloat16)
    rest = value - high.astype(jnp.float32)
    mid = rest.astype(jnp.bfloat16)
    low = (rest - mid.astype(jnp.float32)).astype(jnp.bfloat16)
    return high, mid, low


def pad_rows(rows):
    width = rows[0].shape[1]
    index = lax.broadcasted_iota(jnp.int32, (16, width), 0)
    block = jnp.zeros((16, width), jnp.float32)
    for at, row in enumerate(rows):
        block = jnp.where(index == at, row.astype(jnp.float32), block)
    return block.astype(jnp.bfloat16)


def ones_rows(width):
    index = lax.broadcasted_iota(jnp.int32, (16, width), 0)
    return jnp.where(index < 3, 1.0, 0.0).astype(jnp.bfloat16)


def fold(join, value):
    return functools.reduce(
        join, [value[low : low + SUBLANES] for low in range(0, value.shape[0], SUBLANES)]
    )


def lane_tiles(width):
    return [slice(at, at + LANES) for at in range(0, width, LANES)]


def first_kernel(
    scale, x_hbm, y_hbm, out_ref, far_ref, mine_ref, wide_ref, x_ref, y_ref, left, right, logits, tops, sums, sems
):
    _, rows = x_ref.shape
    columns = y_ref.shape[1]
    block = min(512, columns)
    starts = range(0, columns, block)
    first_copy = pltpu.make_async_copy(x_hbm, x_ref, sems.at[0])
    first_copy.start()
    waits = {}
    count = sems.shape[0] - 1
    for at in range(count):
        span = slice(at * columns // count, (at + 1) * columns // count)
        waits[at * len(starts) // count] = pltpu.make_async_copy(
            y_hbm.at[:, span], y_ref.at[:, span], sems.at[1 + at]
        )
    for copy in waits.values():
        copy.start()
    first_copy.wait()
    x = x_ref[...]
    wide_ref[...] = x.astype(jnp.float32)
    far_ref[...] = scale * jnp.sum(jnp.square(x.astype(jnp.float32)), axis=0, keepdims=True)
    wide = x.astype(jnp.float32) * (2.0 * scale)
    left[...] = jnp.concatenate([*pieces(wide), ones_rows(rows)], axis=0).T
    for at, start in enumerate(starts):
        span = slice(start, start + block)
        if at in waits:
            waits[at].wait()
        piece = y_ref[:, span]
        near = jnp.sum(jnp.square(piece.astype(jnp.float32)), axis=0, keepdims=True)
        right[:, span] = jnp.concatenate(
            [piece, piece, piece, pad_rows(pieces(-scale * near))], axis=0
        )
        part = jnp.dot(left[...], right[:, span], preferred_element_type=jnp.float32)
        logits[:, span] = part
        top = functools.reduce(jnp.maximum, [part[:, tile] for tile in lane_tiles(block)])
        tops[...] = top if start == 0 else jnp.maximum(tops[...], top)
    share = mine_ref.shape[1]
    mine = pl.multiple_of(lax.axis_index("row") * share, share)
    mine_ref[...] = y_ref[:, pl.ds(mine, share)]
    height = min(64, rows)
    for low in range(0, rows, height):
        span = slice(low, low + height)
        top = tops[span, :]
        total = functools.reduce(
            jnp.add, [jnp.exp2(logits[span, tile] - top) for tile in lane_tiles(columns)]
        )
        sums[span, :] = total
    top = tops[...].T
    total = sums[...].T
    peak = jnp.max(top, axis=0, keepdims=True)
    mass = jnp.sum(total * jnp.exp2(top - peak), axis=0, keepdims=True)
    out_ref[...] = peak + jnp.log2(mass)


def logit_block(scale, x_ref, phi_ref, left):
    wide = x_ref[...] * (2.0 * scale)
    left[...] = jnp.concatenate([*pieces(wide), pad_rows(pieces(phi_ref[...]))], axis=0).T


def half_kernel(scale, points, x_ref, phi_ref, y_ref, b_ref, peak_ref, base_ref, right, left):
    columns = b_ref.shape[1]
    block = min(256, columns)
    logit_block(scale, x_ref, phi_ref, left)
    y = y_ref[...]
    right[...] = jnp.concatenate([y, y, y, ones_rows(columns)], axis=0)
    near = jnp.sum(jnp.square(y.astype(jnp.float32)), axis=0, keepdims=True)
    base_ref[...] = scale * near - math.log2(points)
    for start in range(0, columns, block):
        span = slice(start, start + block)
        part = jnp.dot(left[...], right[:, span], preferred_element_type=jnp.float32)
        b_ref[:, span] = part
        peak_ref[:, span] = jnp.max(fold(jnp.maximum, part), axis=0, keepdims=True)


def second_kernel(
    scale, points, b_ref, top_ref, near_ref, right, x_ref, phi_ref, e_ref, r_ref, base_ref, left, part_r
):
    half = b_ref.shape[0]
    cells, columns = e_ref.shape
    block = min(256, columns)
    height = min(64, half)
    logit_block(scale, x_ref, phi_ref, left)
    for start in range(0, columns, block):
        span = slice(start, start + block)
        part = jnp.dot(left[...], right[:, span], preferred_element_type=jnp.float32)
        e_ref[half:, span] = part
        peak = jnp.max(fold(jnp.maximum, part), axis=0, keepdims=True)
        peak = jnp.maximum(peak, top_ref[:, span])
        base_ref[:, span] = near_ref[:, span] - peak
        total = None
        for low in range(0, cells, SUBLANES):
            rows = slice(low, low + SUBLANES)
            expo = jnp.exp2((b_ref if low < half else e_ref)[rows, span] - peak)
            e_ref[rows, span] = expo
            total = expo if total is None else total + expo
        weight = 1.0 / (points * jnp.sum(total, axis=0, keepdims=True))
        for low in range(0, cells, height):
            rows = slice(low, low + height)
            share = e_ref[rows, span] * weight
            row = functools.reduce(jnp.add, [share[:, tile] for tile in lane_tiles(block)])
            part_r[rows, :] = row if start == 0 else part_r[rows, :] + row
    r_ref[...] = jnp.sum(part_r[...].T, axis=0, keepdims=True)


def meet_kernel(own_ref, other_ref, out_ref):
    rows = own_ref.shape[1] // 2
    out_ref[:, :rows] = own_ref[:, :rows] + other_ref[:, rows:]
    out_ref[:, rows:] = own_ref[:, rows:] + other_ref[:, :rows]


def split_kernel(e_ref, after_ref, high_ref, low_ref):
    del after_ref
    height = min(32, e_ref.shape[0])

    @pl.loop(0, e_ref.shape[0] // height)
    def _(at):
        span = pl.ds(pl.multiple_of(at * height, height), height)
        e = e_ref[span, :]
        high = e.astype(jnp.bfloat16)
        high_ref[span, :] = high
        low_ref[span, :] = (e - high.astype(jnp.float32)).astype(jnp.bfloat16)


def weights_kernel(count, own_ref, other_ref, *refs):
    *r_refs, out_ref = refs
    w = 1.0 / (count * functools.reduce(jnp.add, [ref[...] for ref in r_refs]))
    wide = jnp.concatenate([own_ref[...], other_ref[...]], axis=1) * w
    high = wide.astype(jnp.bfloat16)
    low = (wide - high.astype(jnp.float32)).astype(jnp.bfloat16)
    out_ref[...] = jnp.concatenate([high, pad_rows(pieces(w)), low], axis=0)


def third_kernel(key, dims, weights_ref, high_ref, low_ref, base_ref, out_ref, g_ref):
    width = out_ref.shape[1]
    start = 0
    if key is not None:
        start = pl.multiple_of((lax.axis_index("atlas") ^ key) * width, LANES)
    span = pl.ds(start, width)
    upper = dims + 16
    moved = jnp.dot(weights_ref[...], high_ref[:, span], preferred_element_type=jnp.float32)
    rest = jnp.dot(weights_ref[:upper, :], low_ref[:, span], preferred_element_type=jnp.float32)
    mass = jnp.sum(moved[dims:upper, :] + rest[dims:upper, :], axis=0, keepdims=True)
    out_ref[...] = (moved[:dims, :] + moved[upper:, :] + rest[:dims, :]) / mass
    g_ref[...] = (blur / LOG2E) * (base_ref[:, span] - jnp.log2(mass))


def assemble_kernel(atlases, *refs):
    own, other, g_own, g_other = refs[:atlases], refs[atlases : 2 * atlases], *refs[2 * atlases : 2 * atlases + 2]
    out_ref, g_hbm, image, g_ref, sems = refs[2 * atlases + 2 :]
    dims, width = own[0].shape
    atlas = lax.axis_index("atlas")
    row = lax.axis_index("row")
    places = []
    for half, slabs, duals in ((row, own, g_own), (1 - row, other, g_other)):
        for key in range(atlases):
            start = pl.multiple_of((half * atlases + (atlas ^ key)) * width, LANES)
            places.append((slabs[key], start))
            g_ref[:, pl.ds(start, width)] = duals[:, key * width : (key + 1) * width]
    copies = [pltpu.make_async_copy(g_ref, g_hbm, sems.at[0])]
    copies[0].start()
    for low in range(0, dims, SUBLANES):
        rows = slice(low, low + SUBLANES)
        for slab, start in places:
            image[rows, pl.ds(start, width)] = slab[rows, :]
        copies.append(
            pltpu.make_async_copy(image.at[rows, :], out_ref.at[rows, :], sems.at[len(copies)])
        )
        copies[-1].start()
    for copy in copies:
        copy.wait()


def exchange(value, axis, size, key):
    return lax.ppermute(value, axis, [(at, at ^ key) for at in range(size)])


def partners(value, axis):
    size = lax.axis_size(axis)
    if size & (size - 1) == 0 and size <= 8:
        return [exchange(value, axis, size, key) for key in range(1, size)]
    return [
        lax.ppermute(value, axis, [(at, (at + key) % size) for at in range(size)])
        for key in range(1, size)
    ]


def shards(cells, support):
    own = cells[0]
    dims, rows = own.shape
    columns = support.shape[1]
    row_size = lax.axis_size("row")
    atlases = lax.axis_size("atlas")
    total_cells = rows * row_size
    total_support = columns * lax.axis_size("col")
    share = columns // row_size
    scale = LOG2E / (blur * dims)
    row_at = lax.axis_index("row")
    paired = row_size == 2

    def halves(value):
        if paired:
            return value, exchange(value, "row", 2, 1)
        value = lax.all_gather(value, "row", axis=value.ndim - 1, tiled=True)
        return jnp.split(value, 2, axis=-1)

    def sum_rows(value):
        if paired:
            return pl.pallas_call(
                meet_kernel,
                out_shape=jax.ShapeDtypeStruct(value.shape, jnp.float32),
                in_specs=[VMEM, VMEM],
                out_specs=VMEM,
                compiler_params=pltpu.CompilerParams(vmem_limit_bytes=4 << 20),
                name="meet",
            )(value, exchange(value, "row", 2, 1))
        return lax.psum(value, "row")

    def own_rows(value):
        if paired:
            return value[:, :rows]
        return lax.dynamic_slice_in_dim(value, row_at * rows, rows, 1)

    def all_rows(value):
        return lax.all_gather(value, "row", axis=1, tiled=True)

    half = total_cells // 2
    depth = 3 * dims + 16

    def row_vector(width):
        return jax.ShapeDtypeStruct((1, width), jnp.float32)

    lam, far, mine, some = pl.pallas_call(
        functools.partial(first_kernel, scale),
        out_shape=(
            row_vector(rows),
            row_vector(rows),
            jax.ShapeDtypeStruct((dims, share), jnp.bfloat16),
            jax.ShapeDtypeStruct((dims, rows), jnp.float32),
        ),
        in_specs=[HBM, HBM],
        out_specs=(VMEM,) * 4,
        scratch_shapes=[
            pltpu.VMEM((dims, rows), jnp.bfloat16),
            pltpu.VMEM((dims, columns), jnp.bfloat16),
            pltpu.VMEM((rows, depth), jnp.bfloat16),
            pltpu.VMEM((depth, columns), jnp.bfloat16),
            pltpu.VMEM((rows, columns), jnp.float32),
            pltpu.VMEM((rows, LANES), jnp.float32),
            pltpu.VMEM((rows, LANES), jnp.float32),
            pltpu.SemaphoreType.DMA((3 if columns % 1024 == 0 else 2,)),
        ],
        compiler_params=pltpu.CompilerParams(vmem_limit_bytes=24 << 20),
        name="first",
    )(
        pltpu.with_memory_space_constraint(own, pltpu.HBM),
        pltpu.with_memory_space_constraint(support, pltpu.HBM),
    )

    others = partners(lam, "col")
    some, rest = halves(some)
    peak = functools.reduce(jnp.maximum, others, lam)
    mass = functools.reduce(jnp.add, [jnp.exp2(one - peak) for one in [lam, *others]])
    phi = -math.log2(total_cells) - (peak + jnp.log2(mass))

    phi_some, phi_rest = halves(phi)
    logits, tops, near, right = pl.pallas_call(
        functools.partial(half_kernel, scale, float(total_support)),
        out_shape=(
            jax.ShapeDtypeStruct((half, share), jnp.float32),
            row_vector(share),
            row_vector(share),
            jax.ShapeDtypeStruct((depth, share), jnp.bfloat16),
        ),
        in_specs=[VMEM] * 3,
        out_specs=(VMEM,) * 4,
        scratch_shapes=[pltpu.VMEM((half, depth), jnp.bfloat16)],
        compiler_params=pltpu.CompilerParams(vmem_limit_bytes=24 << 20),
        name="half",
    )(some, phi_some, mine)
    e, r, base = pl.pallas_call(
        functools.partial(second_kernel, scale, float(total_support)),
        out_shape=(
            jax.ShapeDtypeStruct((total_cells, share), jnp.float32),
            row_vector(total_cells),
            row_vector(share),
        ),
        in_specs=[VMEM] * 6,
        out_specs=(VMEM, VMEM, VMEM),
        scratch_shapes=[
            pltpu.VMEM((half, depth), jnp.bfloat16),
            pltpu.VMEM((total_cells, LANES), jnp.float32),
        ],
        compiler_params=pltpu.CompilerParams(vmem_limit_bytes=32 << 20),
        name="second",
    )(logits, tops, near, right, rest, phi_rest)

    r = sum_rows(r)
    shares = [r, *partners(r, "col")]

    high, low = pl.pallas_call(
        split_kernel,
        out_shape=(jax.ShapeDtypeStruct(e.shape, jnp.bfloat16),) * 2,
        in_specs=[VMEM, VMEM],
        out_specs=(VMEM, VMEM),
        compiler_params=pltpu.CompilerParams(vmem_limit_bytes=24 << 20),
        cost_estimate=pl.CostEstimate(flops=e.size * 4, bytes_accessed=e.size * 8, transcendentals=0),
        name="split",
    )(e, r)
    weights = pl.pallas_call(
        functools.partial(weights_kernel, float(total_cells)),
        out_shape=jax.ShapeDtypeStruct((2 * dims + 16, total_cells), jnp.bfloat16),
        in_specs=[VMEM] * (2 + len(shares)),
        out_specs=VMEM,
        compiler_params=pltpu.CompilerParams(vmem_limit_bytes=16 << 20),
        name="weights",
    )(some, rest, *shares)

    def third(key, width):
        return pl.pallas_call(
            functools.partial(third_kernel, key, dims),
            out_shape=(jax.ShapeDtypeStruct((dims, width), jnp.float32), row_vector(width)),
            in_specs=[VMEM] * 4,
            out_specs=(VMEM, VMEM),
            compiler_params=pltpu.CompilerParams(vmem_limit_bytes=16 << 20),
            cost_estimate=pl.CostEstimate(
                flops=2 * (3 * dims + 32) * total_cells * width,
                bytes_accessed=4 * total_cells * width,
                transcendentals=0,
            ),
            name="third",
        )(weights, high, low, base)

    piece = share // atlases
    if paired and atlases & (atlases - 1) == 0 and atlases <= 8 and piece % LANES == 0:

        order = [*range(atlases - 1, 0, -1), 0]
        terms, duals, arrived = [None] * atlases, [None] * atlases, []
        for key in order:
            terms[key], duals[key] = third(key, piece)
            if key:
                arrived.append(exchange(terms[key], "atlas", atlases, key))
        sums = functools.reduce(jnp.add, arrived, terms[0]) * (1.0 / atlases)
        slabs = [sums, *partners(sums, "atlas")]
        duals = jnp.concatenate(duals, axis=1)
        updated, dual_g = pl.pallas_call(
            functools.partial(assemble_kernel, atlases),
            out_shape=(jax.ShapeDtypeStruct((dims, columns), jnp.float32), row_vector(columns)),
            in_specs=[VMEM] * (2 * atlases + 2),
            out_specs=(HBM, HBM),
            scratch_shapes=[
                pltpu.VMEM((dims, columns), jnp.float32),
                pltpu.VMEM((1, columns), jnp.float32),
                pltpu.SemaphoreType.DMA((1 + dims // SUBLANES,)),
            ],
            compiler_params=pltpu.CompilerParams(vmem_limit_bytes=8 << 20),
            name="assemble",
        )(
            *slabs,
            *[exchange(slab, "row", 2, 1) for slab in slabs],
            duals,
            exchange(duals, "row", 2, 1),
        )
    else:
        moved, dual_g = third(None, share)
        updated = all_rows(lax.psum(moved, "atlas") * (1.0 / atlases))
        dual_g = all_rows(dual_g)

    cell_dual = (blur / LOG2E) * (
        phi + far - jnp.log2(total_cells * own_rows(functools.reduce(jnp.add, shares)))
    )

    return (cell_dual, dual_g, updated)


def solution(mesh):
    in_specs = (P("atlas", None, "row"), P(None, "col"))
    out_specs = (P("atlas", "row"), P("atlas", "col"), P(None, "col"))
    return jax.shard_map(shards, mesh=mesh, in_specs=in_specs, out_specs=out_specs, check_vma=False)
```

```python
import functools
import math

import jax
import jax.numpy as jnp
from jax import lax
from jax.experimental import pallas as pl
from jax.experimental.pallas import tpu as pltpu
from jax.sharding import PartitionSpec as P


blur = 0.1
LANES = 128
SUBLANES = 8
LOG2E = 1.4426950408889634
VMEM = pl.BlockSpec(memory_space=pltpu.VMEM)
HBM = pl.BlockSpec(memory_space=pltpu.HBM)


def pieces(value):
    high = value.astype(jnp.bfloat16)
    rest = value - high.astype(jnp.float32)
    mid = rest.astype(jnp.bfloat16)
    low = (rest - mid.astype(jnp.float32)).astype(jnp.bfloat16)
    return high, mid, low


def pad_rows(rows):
    width = rows[0].shape[1]
    index = lax.broadcasted_iota(jnp.int32, (16, width), 0)
    block = jnp.zeros((16, width), jnp.float32)
    for at, row in enumerate(rows):
        block = jnp.where(index == at, row.astype(jnp.float32), block)
    return block.astype(jnp.bfloat16)


def ones_rows(width):
    index = lax.broadcasted_iota(jnp.int32, (16, width), 0)
    return jnp.where(index < 3, 1.0, 0.0).astype(jnp.bfloat16)


def fold(join, value):
    return functools.reduce(
        join, [value[low : low + SUBLANES] for low in range(0, value.shape[0], SUBLANES)]
    )


def lane_tiles(width):
    return [slice(at, at + LANES) for at in range(0, width, LANES)]


def first_kernel(
    scale, x_hbm, y_hbm, out_ref, far_ref, mine_ref, wide_ref, x_ref, y_ref, left, right, logits, tops, sums, sems
):
    _, rows = x_ref.shape
    columns = y_ref.shape[1]
    block = min(512, columns)
    starts = range(0, columns, block)
    first_copy = pltpu.make_async_copy(x_hbm, x_ref, sems.at[0])
    first_copy.start()
    waits = {}
    count = sems.shape[0] - 1
    for at in range(count):
        span = slice(at * columns // count, (at + 1) * columns // count)
        waits[at * len(starts) // count] = pltpu.make_async_copy(
            y_hbm.at[:, span], y_ref.at[:, span], sems.at[1 + at]
        )
    for copy in waits.values():
        copy.start()
    first_copy.wait()
    x = x_ref[...]
    wide_ref[...] = x.astype(jnp.float32)
    far_ref[...] = scale * jnp.sum(jnp.square(x.astype(jnp.float32)), axis=0, keepdims=True)
    wide = x.astype(jnp.float32) * (2.0 * scale)
    left[...] = jnp.concatenate([*pieces(wide), ones_rows(rows)], axis=0).T
    for at, start in enumerate(starts):
        span = slice(start, start + block)
        if at in waits:
            waits[at].wait()
        piece = y_ref[:, span]
        near = jnp.sum(jnp.square(piece.astype(jnp.float32)), axis=0, keepdims=True)
        right[:, span] = jnp.concatenate(
            [piece, piece, piece, pad_rows(pieces(-scale * near))], axis=0
        )
        part = jnp.dot(left[...], right[:, span], preferred_element_type=jnp.float32)
        logits[:, span] = part
        top = functools.reduce(jnp.maximum, [part[:, tile] for tile in lane_tiles(block)])
        tops[...] = top if start == 0 else jnp.maximum(tops[...], top)
    share = mine_ref.shape[1]
    mine = pl.multiple_of(lax.axis_index("row") * share, share)
    mine_ref[...] = y_ref[:, pl.ds(mine, share)]
    height = min(64, rows)
    for low in range(0, rows, height):
        span = slice(low, low + height)
        top = tops[span, :]
        total = functools.reduce(
            jnp.add, [jnp.exp2(logits[span, tile] - top) for tile in lane_tiles(columns)]
        )
        sums[span, :] = total
    top = tops[...].T
    total = sums[...].T
    peak = jnp.max(top, axis=0, keepdims=True)
    mass = jnp.sum(total * jnp.exp2(top - peak), axis=0, keepdims=True)
    out_ref[...] = peak + jnp.log2(mass)


def logit_block(scale, x_ref, phi_ref, left):
    wide = x_ref[...] * (2.0 * scale)
    left[...] = jnp.concatenate([*pieces(wide), pad_rows(pieces(phi_ref[...]))], axis=0).T


def exponentials(ref, span, peak):
    total = None
    for low in range(0, ref.shape[0], SUBLANES):
        rows = slice(low, low + SUBLANES)
        expo = jnp.exp2(ref[rows, span] - peak)
        ref[rows, span] = expo
        total = expo if total is None else total + expo
    return jnp.sum(total, axis=0, keepdims=True)


def half_kernel(
    scale, points, x_ref, phi_ref, y_ref, b_ref, peak_ref, sum_ref, base_ref, right, left
):
    columns = b_ref.shape[1]
    block = min(256, columns)
    logit_block(scale, x_ref, phi_ref, left)
    y = y_ref[...]
    right[...] = jnp.concatenate([y, y, y, ones_rows(columns)], axis=0)
    near = jnp.sum(jnp.square(y.astype(jnp.float32)), axis=0, keepdims=True)
    base_ref[...] = scale * near - math.log2(points)
    for start in range(0, columns, block):
        span = slice(start, start + block)
        part = jnp.dot(left[...], right[:, span], preferred_element_type=jnp.float32)
        b_ref[:, span] = part
        peak = jnp.max(fold(jnp.maximum, part), axis=0, keepdims=True)
        peak_ref[:, span] = peak
        sum_ref[:, span] = exponentials(b_ref, span, peak)


def second_kernel(
    scale, points, b_ref, top_ref, sum_ref, near_ref, right, x_ref, phi_ref,
    e_ref, factor_ref, r_ref, base_ref, left, part_r,
):
    half, columns = e_ref.shape
    block = min(256, columns)
    height = min(64, half)
    logit_block(scale, x_ref, phi_ref, left)
    for start in range(0, columns, block):
        span = slice(start, start + block)
        part = jnp.dot(left[...], right[:, span], preferred_element_type=jnp.float32)
        e_ref[:, span] = part
        peak = jnp.max(fold(jnp.maximum, part), axis=0, keepdims=True)
        peak = jnp.maximum(peak, top_ref[:, span])
        base_ref[:, span] = near_ref[:, span] - peak
        factor = jnp.exp2(top_ref[:, span] - peak)
        factor_ref[:, span] = factor
        total = exponentials(e_ref, span, peak) + factor * sum_ref[:, span]
        weight = 1.0 / (points * total)
        for at, (ref, share) in enumerate(((b_ref, factor * weight), (e_ref, weight))):
            for low in range(0, half, height):
                held = ref[low : low + height, span] * share
                row = functools.reduce(jnp.add, [held[:, tile] for tile in lane_tiles(block)])
                rows = slice(at * half + low, at * half + low + height)
                part_r[rows, :] = row if start == 0 else part_r[rows, :] + row
    r_ref[...] = jnp.sum(part_r[...].T, axis=0, keepdims=True)


def meet_kernel(own_ref, other_ref, out_ref):
    rows = own_ref.shape[1] // 2
    out_ref[:, :rows] = own_ref[:, :rows] + other_ref[:, rows:]
    out_ref[:, rows:] = own_ref[:, rows:] + other_ref[:, :rows]


def split_kernel(b_ref, e_ref, factor_ref, after_ref, high_ref, low_ref):
    del after_ref
    half = e_ref.shape[0]
    height = min(32, half)

    def put(at, e):
        span = pl.ds(pl.multiple_of(at, height), height)
        high = e.astype(jnp.bfloat16)
        high_ref[span, :] = high
        low_ref[span, :] = (e - high.astype(jnp.float32)).astype(jnp.bfloat16)

    @pl.loop(0, half // height)
    def _(at):
        low = pl.multiple_of(at * height, height)
        put(low, b_ref[pl.ds(low, height), :] * factor_ref[...])

    @pl.loop(0, half // height)
    def _(at):
        low = pl.multiple_of(at * height, height)
        put(half + low, e_ref[pl.ds(low, height), :])


def weights_kernel(count, own_ref, other_ref, *refs):
    *r_refs, out_ref = refs
    w = 1.0 / (count * functools.reduce(jnp.add, [ref[...] for ref in r_refs]))
    wide = jnp.concatenate([own_ref[...], other_ref[...]], axis=1) * w
    high = wide.astype(jnp.bfloat16)
    low = (wide - high.astype(jnp.float32)).astype(jnp.bfloat16)
    out_ref[...] = jnp.concatenate([high, pad_rows(pieces(w)), low], axis=0)


def third_kernel(key, dims, weights_ref, high_ref, low_ref, base_ref, out_ref, g_ref):
    width = out_ref.shape[1]
    start = 0
    if key is not None:
        start = pl.multiple_of((lax.axis_index("atlas") ^ key) * width, LANES)
    span = pl.ds(start, width)
    upper = dims + 16
    moved = jnp.dot(weights_ref[...], high_ref[:, span], preferred_element_type=jnp.float32)
    rest = jnp.dot(weights_ref[:upper, :], low_ref[:, span], preferred_element_type=jnp.float32)
    mass = jnp.sum(moved[dims:upper, :] + rest[dims:upper, :], axis=0, keepdims=True)
    out_ref[...] = (moved[:dims, :] + moved[upper:, :] + rest[:dims, :]) / mass
    g_ref[...] = (blur / LOG2E) * (base_ref[:, span] - jnp.log2(mass))


def assemble_kernel(atlases, *refs):
    own, other, g_own, g_other = refs[:atlases], refs[atlases : 2 * atlases], *refs[2 * atlases : 2 * atlases + 2]
    out_ref, g_hbm, image, g_ref, sems = refs[2 * atlases + 2 :]
    dims, width = own[0].shape
    atlas = lax.axis_index("atlas")
    row = lax.axis_index("row")
    places = []
    for half, slabs, duals in ((row, own, g_own), (1 - row, other, g_other)):
        for key in range(atlases):
            start = pl.multiple_of((half * atlases + (atlas ^ key)) * width, LANES)
            places.append((slabs[key], start))
            g_ref[:, pl.ds(start, width)] = duals[:, key * width : (key + 1) * width]
    copies = [pltpu.make_async_copy(g_ref, g_hbm, sems.at[0])]
    copies[0].start()
    for low in range(0, dims, SUBLANES):
        rows = slice(low, low + SUBLANES)
        for slab, start in places:
            image[rows, pl.ds(start, width)] = slab[rows, :]
        copies.append(
            pltpu.make_async_copy(image.at[rows, :], out_ref.at[rows, :], sems.at[len(copies)])
        )
        copies[-1].start()
    for copy in copies:
        copy.wait()


def exchange(value, axis, size, key):
    return lax.ppermute(value, axis, [(at, at ^ key) for at in range(size)])


def partners(value, axis):
    size = lax.axis_size(axis)
    if size & (size - 1) == 0 and size <= 8:
        return [exchange(value, axis, size, key) for key in range(1, size)]
    return [
        lax.ppermute(value, axis, [(at, (at + key) % size) for at in range(size)])
        for key in range(1, size)
    ]


def shards(cells, support):
    own = cells[0]
    dims, rows = own.shape
    columns = support.shape[1]
    row_size = lax.axis_size("row")
    atlases = lax.axis_size("atlas")
    total_cells = rows * row_size
    total_support = columns * lax.axis_size("col")
    share = columns // row_size
    scale = LOG2E / (blur * dims)
    row_at = lax.axis_index("row")
    paired = row_size == 2

    def halves(value):
        if paired:
            return value, exchange(value, "row", 2, 1)
        value = lax.all_gather(value, "row", axis=value.ndim - 1, tiled=True)
        return jnp.split(value, 2, axis=-1)

    def sum_rows(value):
        if paired:
            return pl.pallas_call(
                meet_kernel,
                out_shape=jax.ShapeDtypeStruct(value.shape, jnp.float32),
                in_specs=[VMEM, VMEM],
                out_specs=VMEM,
                compiler_params=pltpu.CompilerParams(vmem_limit_bytes=4 << 20),
                name="meet",
            )(value, exchange(value, "row", 2, 1))
        return lax.psum(value, "row")

    def own_rows(value):
        if paired:
            return value[:, :rows]
        return lax.dynamic_slice_in_dim(value, row_at * rows, rows, 1)

    def all_rows(value):
        return lax.all_gather(value, "row", axis=1, tiled=True)

    half = total_cells // 2
    depth = 3 * dims + 16

    def row_vector(width):
        return jax.ShapeDtypeStruct((1, width), jnp.float32)

    lam, far, mine, some = pl.pallas_call(
        functools.partial(first_kernel, scale),
        out_shape=(
            row_vector(rows),
            row_vector(rows),
            jax.ShapeDtypeStruct((dims, share), jnp.bfloat16),
            jax.ShapeDtypeStruct((dims, rows), jnp.float32),
        ),
        in_specs=[HBM, HBM],
        out_specs=(VMEM,) * 4,
        scratch_shapes=[
            pltpu.VMEM((dims, rows), jnp.bfloat16),
            pltpu.VMEM((dims, columns), jnp.bfloat16),
            pltpu.VMEM((rows, depth), jnp.bfloat16),
            pltpu.VMEM((depth, columns), jnp.bfloat16),
            pltpu.VMEM((rows, columns), jnp.float32),
            pltpu.VMEM((rows, LANES), jnp.float32),
            pltpu.VMEM((rows, LANES), jnp.float32),
            pltpu.SemaphoreType.DMA((3 if columns % 1024 == 0 else 2,)),
        ],
        compiler_params=pltpu.CompilerParams(vmem_limit_bytes=24 << 20),
        name="first",
    )(
        pltpu.with_memory_space_constraint(own, pltpu.HBM),
        pltpu.with_memory_space_constraint(support, pltpu.HBM),
    )

    others = partners(lam, "col")
    some, rest = halves(some)
    peak = functools.reduce(jnp.maximum, others, lam)
    mass = functools.reduce(jnp.add, [jnp.exp2(one - peak) for one in [lam, *others]])
    phi = -math.log2(total_cells) - (peak + jnp.log2(mass))

    phi_some, phi_rest = halves(phi)
    some_e, tops, masses, near, right = pl.pallas_call(
        functools.partial(half_kernel, scale, float(total_support)),
        out_shape=(
            jax.ShapeDtypeStruct((half, share), jnp.float32),
            row_vector(share),
            row_vector(share),
            row_vector(share),
            jax.ShapeDtypeStruct((depth, share), jnp.bfloat16),
        ),
        in_specs=[VMEM] * 3,
        out_specs=(VMEM,) * 5,
        scratch_shapes=[pltpu.VMEM((half, depth), jnp.bfloat16)],
        compiler_params=pltpu.CompilerParams(vmem_limit_bytes=24 << 20),
        name="half",
    )(some, phi_some, mine)
    rest_e, factor, r, base = pl.pallas_call(
        functools.partial(second_kernel, scale, float(total_support)),
        out_shape=(
            jax.ShapeDtypeStruct((half, share), jnp.float32),
            row_vector(share),
            row_vector(total_cells),
            row_vector(share),
        ),
        in_specs=[VMEM] * 7,
        out_specs=(VMEM,) * 4,
        scratch_shapes=[
            pltpu.VMEM((half, depth), jnp.bfloat16),
            pltpu.VMEM((total_cells, LANES), jnp.float32),
        ],
        compiler_params=pltpu.CompilerParams(vmem_limit_bytes=32 << 20),
        name="second",
    )(some_e, tops, masses, near, right, rest, phi_rest)

    r = sum_rows(r)
    shares = [r, *partners(r, "col")]

    high, low = pl.pallas_call(
        split_kernel,
        out_shape=(jax.ShapeDtypeStruct((total_cells, share), jnp.bfloat16),) * 2,
        in_specs=[VMEM] * 4,
        out_specs=(VMEM, VMEM),
        compiler_params=pltpu.CompilerParams(vmem_limit_bytes=24 << 20),
        cost_estimate=pl.CostEstimate(flops=total_cells * share * 4, bytes_accessed=total_cells * share * 8, transcendentals=0),
        name="split",
    )(some_e, rest_e, factor, r)
    weights = pl.pallas_call(
        functools.partial(weights_kernel, float(total_cells)),
        out_shape=jax.ShapeDtypeStruct((2 * dims + 16, total_cells), jnp.bfloat16),
        in_specs=[VMEM] * (2 + len(shares)),
        out_specs=VMEM,
        compiler_params=pltpu.CompilerParams(vmem_limit_bytes=16 << 20),
        name="weights",
    )(some, rest, *shares)

    def third(key, width):
        return pl.pallas_call(
            functools.partial(third_kernel, key, dims),
            out_shape=(jax.ShapeDtypeStruct((dims, width), jnp.float32), row_vector(width)),
            in_specs=[VMEM] * 4,
            out_specs=(VMEM, VMEM),
            compiler_params=pltpu.CompilerParams(vmem_limit_bytes=16 << 20),
            cost_estimate=pl.CostEstimate(
                flops=2 * (3 * dims + 32) * total_cells * width,
                bytes_accessed=4 * total_cells * width,
                transcendentals=0,
            ),
            name="third",
        )(weights, high, low, base)

    piece = share // atlases
    if paired and atlases & (atlases - 1) == 0 and atlases <= 8 and piece % LANES == 0:

        order = [*range(atlases - 1, 0, -1), 0]
        terms, duals, arrived = [None] * atlases, [None] * atlases, []
        for key in order:
            terms[key], duals[key] = third(key, piece)
            if key:
                arrived.append(exchange(terms[key], "atlas", atlases, key))
        sums = functools.reduce(jnp.add, arrived, terms[0]) * (1.0 / atlases)
        slabs = [sums, *partners(sums, "atlas")]
        duals = jnp.concatenate(duals, axis=1)
        updated, dual_g = pl.pallas_call(
            functools.partial(assemble_kernel, atlases),
            out_shape=(jax.ShapeDtypeStruct((dims, columns), jnp.float32), row_vector(columns)),
            in_specs=[VMEM] * (2 * atlases + 2),
            out_specs=(HBM, HBM),
            scratch_shapes=[
                pltpu.VMEM((dims, columns), jnp.float32),
                pltpu.VMEM((1, columns), jnp.float32),
                pltpu.SemaphoreType.DMA((1 + dims // SUBLANES,)),
            ],
            compiler_params=pltpu.CompilerParams(vmem_limit_bytes=8 << 20),
            name="assemble",
        )(
            *slabs,
            *[exchange(slab, "row", 2, 1) for slab in slabs],
            duals,
            exchange(duals, "row", 2, 1),
        )
    else:
        moved, dual_g = third(None, share)
        updated = all_rows(lax.psum(moved, "atlas") * (1.0 / atlases))
        dual_g = all_rows(dual_g)

    cell_dual = (blur / LOG2E) * (
        phi + far - jnp.log2(total_cells * own_rows(functools.reduce(jnp.add, shares)))
    )

    return (cell_dual, dual_g, updated)


def solution(mesh):
    in_specs = (P("atlas", None, "row"), P(None, "col"))
    out_specs = (P("atlas", "row"), P("atlas", "col"), P(None, "col"))
    return jax.shard_map(shards, mesh=mesh, in_specs=in_specs, out_specs=out_specs, check_vma=False)
```

```python
import functools
import math

import jax
import jax.numpy as jnp
from jax import lax
from jax.experimental import pallas as pl
from jax.experimental.pallas import tpu as pltpu
from jax.sharding import PartitionSpec as P


blur = 0.1
LANES = 128
SUBLANES = 8
LOG2E = 1.4426950408889634
VMEM = pl.BlockSpec(memory_space=pltpu.VMEM)
HBM = pl.BlockSpec(memory_space=pltpu.HBM)


def pieces(value):
    high = value.astype(jnp.bfloat16)
    rest = value - high.astype(jnp.float32)
    mid = rest.astype(jnp.bfloat16)
    low = (rest - mid.astype(jnp.float32)).astype(jnp.bfloat16)
    return high, mid, low


def pad_rows(rows):
    width = rows[0].shape[1]
    index = lax.broadcasted_iota(jnp.int32, (16, width), 0)
    block = jnp.zeros((16, width), jnp.float32)
    for at, row in enumerate(rows):
        block = jnp.where(index == at, row.astype(jnp.float32), block)
    return block.astype(jnp.bfloat16)


def ones_rows(width):
    index = lax.broadcasted_iota(jnp.int32, (16, width), 0)
    return jnp.where(index < 3, 1.0, 0.0).astype(jnp.bfloat16)


def fold(join, value):
    return functools.reduce(
        join, [value[low : low + SUBLANES] for low in range(0, value.shape[0], SUBLANES)]
    )


def lane_tiles(width):
    return [slice(at, at + LANES) for at in range(0, width, LANES)]


def first_kernel(
    scale, x_hbm, y_hbm, out_ref, far_ref, mine_ref, wide_ref, x_ref, y_ref, left, right, logits, tops, sums, sems
):
    _, rows = x_ref.shape
    columns = y_ref.shape[1]
    block = min(512, columns)
    starts = range(0, columns, block)
    first_copy = pltpu.make_async_copy(x_hbm, x_ref, sems.at[0])
    first_copy.start()
    waits = {}
    count = sems.shape[0] - 1
    for at in range(count):
        span = slice(at * columns // count, (at + 1) * columns // count)
        waits[at * len(starts) // count] = pltpu.make_async_copy(
            y_hbm.at[:, span], y_ref.at[:, span], sems.at[1 + at]
        )
    for copy in waits.values():
        copy.start()
    first_copy.wait()
    x = x_ref[...]
    wide_ref[...] = x.astype(jnp.float32)
    far_ref[...] = scale * jnp.sum(jnp.square(x.astype(jnp.float32)), axis=0, keepdims=True)
    wide = x.astype(jnp.float32) * (2.0 * scale)
    left[...] = jnp.concatenate([*pieces(wide), ones_rows(rows)], axis=0).T
    for at, start in enumerate(starts):
        span = slice(start, start + block)
        if at in waits:
            waits[at].wait()
        piece = y_ref[:, span]
        near = jnp.sum(jnp.square(piece.astype(jnp.float32)), axis=0, keepdims=True)
        right[:, span] = jnp.concatenate(
            [piece, piece, piece, pad_rows(pieces(-scale * near))], axis=0
        )
        part = jnp.dot(left[...], right[:, span], preferred_element_type=jnp.float32)
        logits[:, span] = part
        top = functools.reduce(jnp.maximum, [part[:, tile] for tile in lane_tiles(block)])
        tops[...] = top if start == 0 else jnp.maximum(tops[...], top)
    share = mine_ref.shape[1]
    mine = pl.multiple_of(lax.axis_index("row") * share, share)
    mine_ref[...] = y_ref[:, pl.ds(mine, share)]
    height = min(64, rows)
    for low in range(0, rows, height):
        span = slice(low, low + height)
        top = tops[span, :]
        total = functools.reduce(
            jnp.add, [jnp.exp2(logits[span, tile] - top) for tile in lane_tiles(columns)]
        )
        sums[span, :] = total
    top = tops[...].T
    total = sums[...].T
    peak = jnp.max(top, axis=0, keepdims=True)
    mass = jnp.sum(total * jnp.exp2(top - peak), axis=0, keepdims=True)
    out_ref[...] = peak + jnp.log2(mass)


def logit_block(scale, x_ref, phi_ref, left):
    wide = x_ref[...] * (2.0 * scale)
    left[...] = jnp.concatenate([*pieces(wide), pad_rows(pieces(phi_ref[...]))], axis=0).T


def exponentials(ref, span, peak):
    total = None
    for low in range(0, ref.shape[0], SUBLANES):
        rows = slice(low, low + SUBLANES)
        expo = jnp.exp2(ref[rows, span] - peak)
        ref[rows, span] = expo
        total = expo if total is None else total + expo
    return jnp.sum(total, axis=0, keepdims=True)


def half_kernel(
    scale, points, x_ref, phi_ref, y_ref, b_ref, peak_ref, sum_ref, base_ref, right, left
):
    columns = b_ref.shape[1]
    block = min(512, columns)
    logit_block(scale, x_ref, phi_ref, left)
    y = y_ref[...]
    right[...] = jnp.concatenate([y, y, y, ones_rows(columns)], axis=0)
    near = jnp.sum(jnp.square(y.astype(jnp.float32)), axis=0, keepdims=True)
    base_ref[...] = scale * near - math.log2(points)
    for start in range(0, columns, block):
        span = slice(start, start + block)
        part = jnp.dot(left[...], right[:, span], preferred_element_type=jnp.float32)
        b_ref[:, span] = part
        peak = jnp.max(fold(jnp.maximum, part), axis=0, keepdims=True)
        peak_ref[:, span] = peak
        sum_ref[:, span] = exponentials(b_ref, span, peak)


def second_kernel(
    scale, points, b_ref, top_ref, sum_ref, near_ref, right, x_ref, phi_ref,
    e_ref, factor_ref, r_ref, base_ref, left, part_r,
):
    half, columns = e_ref.shape
    block = min(512, columns)
    height = min(64, half)
    logit_block(scale, x_ref, phi_ref, left)
    for start in range(0, columns, block):
        span = slice(start, start + block)
        part = jnp.dot(left[...], right[:, span], preferred_element_type=jnp.float32)
        e_ref[:, span] = part
        peak = jnp.max(fold(jnp.maximum, part), axis=0, keepdims=True)
        peak = jnp.maximum(peak, top_ref[:, span])
        base_ref[:, span] = near_ref[:, span] - peak
        factor = jnp.exp2(top_ref[:, span] - peak)
        factor_ref[:, span] = factor
        total = exponentials(e_ref, span, peak) + factor * sum_ref[:, span]
        weight = 1.0 / (points * total)
        for at, (ref, share) in enumerate(((b_ref, factor * weight), (e_ref, weight))):
            for low in range(0, half, height):
                held = ref[low : low + height, span] * share
                row = functools.reduce(jnp.add, [held[:, tile] for tile in lane_tiles(block)])
                rows = slice(at * half + low, at * half + low + height)
                part_r[rows, :] = row if start == 0 else part_r[rows, :] + row
    r_ref[...] = jnp.sum(part_r[...].T, axis=0, keepdims=True)


def meet_kernel(own_ref, other_ref, out_ref):
    rows = own_ref.shape[1] // 2
    out_ref[:, :rows] = own_ref[:, :rows] + other_ref[:, rows:]
    out_ref[:, rows:] = own_ref[:, rows:] + other_ref[:, :rows]


def split_kernel(b_ref, e_ref, factor_ref, after_ref, high_ref, low_ref):
    del after_ref
    half = e_ref.shape[0]
    height = min(32, half)

    def put(at, e):
        span = pl.ds(pl.multiple_of(at, height), height)
        high = e.astype(jnp.bfloat16)
        high_ref[span, :] = high
        low_ref[span, :] = (e - high.astype(jnp.float32)).astype(jnp.bfloat16)

    @pl.loop(0, half // height)
    def _(at):
        low = pl.multiple_of(at * height, height)
        put(low, b_ref[pl.ds(low, height), :] * factor_ref[...])

    @pl.loop(0, half // height)
    def _(at):
        low = pl.multiple_of(at * height, height)
        put(half + low, e_ref[pl.ds(low, height), :])


def weights_kernel(count, own_ref, other_ref, *refs):
    *r_refs, out_ref = refs
    w = 1.0 / (count * functools.reduce(jnp.add, [ref[...] for ref in r_refs]))
    wide = jnp.concatenate([own_ref[...], other_ref[...]], axis=1) * w
    high = wide.astype(jnp.bfloat16)
    low = (wide - high.astype(jnp.float32)).astype(jnp.bfloat16)
    out_ref[...] = jnp.concatenate([high, pad_rows(pieces(w)), low], axis=0)


def third_kernel(key, dims, weights_ref, high_ref, low_ref, base_ref, out_ref, g_ref):
    width = out_ref.shape[1]
    start = 0
    if key is not None:
        start = pl.multiple_of((lax.axis_index("atlas") ^ key) * width, LANES)
    span = pl.ds(start, width)
    upper = dims + 16
    moved = jnp.dot(weights_ref[...], high_ref[:, span], preferred_element_type=jnp.float32)
    rest = jnp.dot(weights_ref[:upper, :], low_ref[:, span], preferred_element_type=jnp.float32)
    mass = jnp.sum(moved[dims:upper, :] + rest[dims:upper, :], axis=0, keepdims=True)
    out_ref[...] = (moved[:dims, :] + moved[upper:, :] + rest[:dims, :]) / mass
    g_ref[...] = (blur / LOG2E) * (base_ref[:, span] - jnp.log2(mass))


def slab_span(half, key, atlases, width):
    slab = half * atlases + (lax.axis_index("atlas") ^ key)
    return pl.ds(pl.multiple_of(slab * width, LANES), width)


def copy_all(copies):
    for copy in copies:
        copy.start()
    for copy in copies:
        copy.wait()


def early_kernel(order, *refs):
    atlases = len(order)
    slabs = refs[: atlases + 1]
    g_own, g_other, out_hbm, g_hbm, g_ref, sems = refs[atlases + 1 :]
    width = slabs[0].shape[1]
    row = lax.axis_index("row")
    places = [(row, key) for key in range(atlases)] + [(1 - row, 0)]
    for half, duals in ((row, g_own), (1 - row, g_other)):
        for at, key in enumerate(order):
            span = slab_span(half, key, atlases, width)
            g_ref[:, span] = duals[:, at * width : (at + 1) * width]
    copies = [pltpu.make_async_copy(g_ref, g_hbm, sems.at[0])]
    for slab, (half, key) in zip(slabs, places):
        target = out_hbm.at[:, slab_span(half, key, atlases, width)]
        copies.append(pltpu.make_async_copy(slab, target, sems.at[len(copies)]))
    copy_all(copies)


def late_kernel(atlases, *refs):
    *slabs, in_hbm, out_hbm, sems = refs
    del in_hbm
    width = slabs[0].shape[1]
    copies = []
    for key, slab in enumerate(slabs, 1):
        target = out_hbm.at[:, slab_span(1 - lax.axis_index("row"), key, atlases, width)]
        copies.append(pltpu.make_async_copy(slab, target, sems.at[key - 1]))
    copy_all(copies)


def exchange(value, axis, size, key):
    return lax.ppermute(value, axis, [(at, at ^ key) for at in range(size)])


def partners(value, axis):
    size = lax.axis_size(axis)
    if size & (size - 1) == 0 and size <= 8:
        return [exchange(value, axis, size, key) for key in range(1, size)]
    return [
        lax.ppermute(value, axis, [(at, (at + key) % size) for at in range(size)])
        for key in range(1, size)
    ]


def shards(cells, support):
    own = cells[0]
    dims, rows = own.shape
    columns = support.shape[1]
    row_size = lax.axis_size("row")
    atlases = lax.axis_size("atlas")
    total_cells = rows * row_size
    total_support = columns * lax.axis_size("col")
    share = columns // row_size
    scale = LOG2E / (blur * dims)
    row_at = lax.axis_index("row")
    paired = row_size == 2

    def halves(value):
        if paired:
            return value, exchange(value, "row", 2, 1)
        value = lax.all_gather(value, "row", axis=value.ndim - 1, tiled=True)
        return jnp.split(value, 2, axis=-1)

    def sum_rows(value):
        if paired:
            return pl.pallas_call(
                meet_kernel,
                out_shape=jax.ShapeDtypeStruct(value.shape, jnp.float32),
                in_specs=[VMEM, VMEM],
                out_specs=VMEM,
                compiler_params=pltpu.CompilerParams(vmem_limit_bytes=4 << 20),
                name="meet",
            )(value, exchange(value, "row", 2, 1))
        return lax.psum(value, "row")

    def own_rows(value):
        if paired:
            return value[:, :rows]
        return lax.dynamic_slice_in_dim(value, row_at * rows, rows, 1)

    def all_rows(value):
        return lax.all_gather(value, "row", axis=1, tiled=True)

    half = total_cells // 2
    depth = 3 * dims + 16

    def row_vector(width):
        return jax.ShapeDtypeStruct((1, width), jnp.float32)

    lam, far, mine, some = pl.pallas_call(
        functools.partial(first_kernel, scale),
        out_shape=(
            row_vector(rows),
            row_vector(rows),
            jax.ShapeDtypeStruct((dims, share), jnp.bfloat16),
            jax.ShapeDtypeStruct((dims, rows), jnp.float32),
        ),
        in_specs=[HBM, HBM],
        out_specs=(VMEM,) * 4,
        scratch_shapes=[
            pltpu.VMEM((dims, rows), jnp.bfloat16),
            pltpu.VMEM((dims, columns), jnp.bfloat16),
            pltpu.VMEM((rows, depth), jnp.bfloat16),
            pltpu.VMEM((depth, columns), jnp.bfloat16),
            pltpu.VMEM((rows, columns), jnp.float32),
            pltpu.VMEM((rows, LANES), jnp.float32),
            pltpu.VMEM((rows, LANES), jnp.float32),
            pltpu.SemaphoreType.DMA((3 if columns % 1024 == 0 else 2,)),
        ],
        compiler_params=pltpu.CompilerParams(vmem_limit_bytes=24 << 20),
        name="first",
    )(
        pltpu.with_memory_space_constraint(own, pltpu.HBM),
        pltpu.with_memory_space_constraint(support, pltpu.HBM),
    )

    others = partners(lam, "col")
    some, rest = halves(some)
    peak = functools.reduce(jnp.maximum, others, lam)
    mass = functools.reduce(jnp.add, [jnp.exp2(one - peak) for one in [lam, *others]])
    phi = -math.log2(total_cells) - (peak + jnp.log2(mass))

    phi_some, phi_rest = halves(phi)
    some_e, tops, masses, near, right = pl.pallas_call(
        functools.partial(half_kernel, scale, float(total_support)),
        out_shape=(
            jax.ShapeDtypeStruct((half, share), jnp.float32),
            row_vector(share),
            row_vector(share),
            row_vector(share),
            jax.ShapeDtypeStruct((depth, share), jnp.bfloat16),
        ),
        in_specs=[VMEM] * 3,
        out_specs=(VMEM,) * 5,
        scratch_shapes=[pltpu.VMEM((half, depth), jnp.bfloat16)],
        compiler_params=pltpu.CompilerParams(vmem_limit_bytes=24 << 20),
        name="half",
    )(some, phi_some, mine)
    rest_e, factor, r, base = pl.pallas_call(
        functools.partial(second_kernel, scale, float(total_support)),
        out_shape=(
            jax.ShapeDtypeStruct((half, share), jnp.float32),
            row_vector(share),
            row_vector(total_cells),
            row_vector(share),
        ),
        in_specs=[VMEM] * 7,
        out_specs=(VMEM,) * 4,
        scratch_shapes=[
            pltpu.VMEM((half, depth), jnp.bfloat16),
            pltpu.VMEM((total_cells, LANES), jnp.float32),
        ],
        compiler_params=pltpu.CompilerParams(vmem_limit_bytes=32 << 20),
        name="second",
    )(some_e, tops, masses, near, right, rest, phi_rest)

    r = sum_rows(r)
    shares = [r, *partners(r, "col")]

    high, low = pl.pallas_call(
        split_kernel,
        out_shape=(jax.ShapeDtypeStruct((total_cells, share), jnp.bfloat16),) * 2,
        in_specs=[VMEM] * 4,
        out_specs=(VMEM, VMEM),
        compiler_params=pltpu.CompilerParams(vmem_limit_bytes=24 << 20),
        cost_estimate=pl.CostEstimate(flops=total_cells * share * 4, bytes_accessed=total_cells * share * 8, transcendentals=0),
        name="split",
    )(some_e, rest_e, factor, r)
    weights = pl.pallas_call(
        functools.partial(weights_kernel, float(total_cells)),
        out_shape=jax.ShapeDtypeStruct((2 * dims + 16, total_cells), jnp.bfloat16),
        in_specs=[VMEM] * (2 + len(shares)),
        out_specs=VMEM,
        compiler_params=pltpu.CompilerParams(vmem_limit_bytes=16 << 20),
        name="weights",
    )(some, rest, *shares)

    def third(key, width):
        return pl.pallas_call(
            functools.partial(third_kernel, key, dims),
            out_shape=(jax.ShapeDtypeStruct((dims, width), jnp.float32), row_vector(width)),
            in_specs=[VMEM] * 4,
            out_specs=(VMEM, VMEM),
            compiler_params=pltpu.CompilerParams(vmem_limit_bytes=16 << 20),
            cost_estimate=pl.CostEstimate(
                flops=2 * (3 * dims + 32) * total_cells * width,
                bytes_accessed=4 * total_cells * width,
                transcendentals=0,
            ),
            name="third",
        )(weights, high, low, base)

    piece = share // atlases
    if paired and atlases & (atlases - 1) == 0 and atlases <= 8 and piece % LANES == 0:

        order = [*range(atlases - 1, 0, -1), 0]
        terms, duals, arrived = [None] * atlases, [None] * atlases, []
        for key in order:
            terms[key], duals[key] = third(key, piece)
            if key:
                arrived.append(exchange(terms[key], "atlas", atlases, key))
        sums = functools.reduce(jnp.add, arrived, terms[0]) * (1.0 / atlases)
        slabs = [sums]
        for key in range(1, atlases):
            slabs.append(exchange(sums, "atlas", atlases, key))
        duals = jnp.concatenate([duals[key] for key in order], axis=1)
        other = []
        for slab in slabs:
            other.append(exchange(slab, "row", 2, 1))
        duals_other = exchange(duals, "row", 2, 1)
        updated, dual_g = pl.pallas_call(
            functools.partial(early_kernel, order),
            out_shape=(jax.ShapeDtypeStruct((dims, columns), jnp.float32), row_vector(columns)),
            in_specs=[VMEM] * (atlases + 3),
            out_specs=(HBM, HBM),
            scratch_shapes=[
                pltpu.VMEM((1, columns), jnp.float32),
                pltpu.SemaphoreType.DMA((atlases + 2,)),
            ],
            compiler_params=pltpu.CompilerParams(vmem_limit_bytes=8 << 20),
            name="early",
        )(*slabs, other[0], duals, duals_other)
        updated = pl.pallas_call(
            functools.partial(late_kernel, atlases),
            out_shape=jax.ShapeDtypeStruct((dims, columns), jnp.float32),
            in_specs=[VMEM] * (atlases - 1) + [HBM],
            out_specs=HBM,
            scratch_shapes=[pltpu.SemaphoreType.DMA((atlases - 1,))],
            input_output_aliases={atlases - 1: 0},
            compiler_params=pltpu.CompilerParams(vmem_limit_bytes=8 << 20),
            name="late",
        )(*other[1:], updated)
    else:
        moved, dual_g = third(None, share)
        updated = all_rows(lax.psum(moved, "atlas") * (1.0 / atlases))
        dual_g = all_rows(dual_g)

    cell_dual = (blur / LOG2E) * (
        phi + far - jnp.log2(total_cells * own_rows(functools.reduce(jnp.add, shares)))
    )

    return (cell_dual, dual_g, updated)


def solution(mesh):
    in_specs = (P("atlas", None, "row"), P(None, "col"))
    out_specs = (P("atlas", "row"), P("atlas", "col"), P(None, "col"))
    return jax.shard_map(shards, mesh=mesh, in_specs=in_specs, out_specs=out_specs, check_vma=False)
```
